1024 devices in a mesh: dp: 16 (over z_hi, x), pipe: 8 (over z_lo, core), seq: 8 (over y).
Axes of the slice: x: 4, y: 8, z: 16 (z_hi: 4, z_lo: 4; z = z_hi * 4 + z_lo), core: 2. Of those that a mesh axis runs over, the one named last changes fastest.
Arguments:
- fwd_input: bfloat16 [8, 16, 1024, 2048], P('pipe', 'dp', 'seq'), may hold values from -6 to 6
- saved_input: bfloat16 [8, 16, 1024, 2048], P('pipe', 'dp', 'seq'), may hold values from -6 to 6
- out_grad: bfloat16 [8, 16, 1024, 2048], P('pipe', 'dp', 'seq'), may hold values from -6 to 6
- fwd_sky: int32 [8, 16, 1024], P('pipe', 'dp'), may hold values 0 or 1
- bwd_sky: int32 [8, 16, 1024], P('pipe', 'dp'), may hold values 0 or 1
- norm_gain: float32 [8, 2048], P('pipe'), may hold values from 0.5 to 1.5
- query_scale: float32 [8, 2048], P('pipe'), may hold values from -4 to 4
- key_scale: float32 [8, 2048], P('pipe'), may hold values from -4 to 4
- value_scale: float32 [8, 2048], P('pipe'), may hold values from -4 to 4
- sky_bias: float32 [8, 16], P('pipe'), may hold values from -4 to 2
Outputs:
- fwd_output: bfloat16 [8, 16, 1024, 2048], P('pipe', 'dp', 'seq')
- bwd_output: bfloat16 [8, 16, 1024, 2048], P('pipe', 'dp', 'seq')
- scale_grads: float32 [8, 4, 2048], P('pipe', None, 'seq')
- bias_grad: float32 [8, 16], P('pipe', 'seq')
The draws below stay inside these ranges and needn't reach their ends.
All inputs are finite; a program needn't handle non-finite values. No bound on the sum of `fwd_sky` or of `bwd_sky` on one device may be relied on, other than what follows from the above.
Results may differ from the reference program's by a relative error of at most 0.0085.
The reference program's roundings to bfloat16 on the way count: a program that leaves them out, or rounds other values in their place, can miss the bound.
Values may be sent and summed in bfloat16 or wider, within the bound.
A program may use at most 32 MiB of HBM per device.

```python
import math
import jax
import jax.numpy as jnp
from jax import lax

D = 2048
HEADS = 16
HEAD_DIM = 128
SEQ_LEN = 1024
SECTIONS = 8
BATCH = 16


def draw_query_scale(key, part):
    drawn = jax.random.normal(jax.random.fold_in(key, 103), (SECTIONS, D), jnp.float32)
    return jnp.clip(drawn, -4.0, 4.0)


def draw_key_scale(key, part):
    drawn = jax.random.normal(jax.random.fold_in(key, 104), (SECTIONS, D), jnp.float32)
    return jnp.clip(drawn, -4.0, 4.0)


def draw_fwd_input(key, part):
    drawn = jax.random.normal(jax.random.fold_in(key, 301), (SECTIONS, BATCH, SEQ_LEN, D), jnp.float32)
    return jnp.clip(drawn, -6.0, 6.0).astype(jnp.bfloat16)


def draw_saved_input(key, part):
    drawn = jax.random.normal(jax.random.fold_in(key, 302), (SECTIONS, BATCH, SEQ_LEN, D), jnp.float32)
    return jnp.clip(drawn, -6.0, 6.0).astype(jnp.bfloat16)


def touch_ends(drawn, stream_key, low, top_value):
    shape = drawn.shape
    place = [jax.random.randint(jax.random.fold_in(stream_key, axis), (), 0, shape[axis]) for axis in range(len(shape))]
    drawn = drawn.at[tuple(place)].set(low)
    longest = shape.index(max(shape))
    place[longest] = (place[longest] + 1) % shape[longest]
    return drawn.at[tuple(place)].set(top_value)


def shard_levels(key, shape, cuts, smallest, high):
    level, own = 1.0, jax.random.fold_in(key, 6)
    for dim, shards_of in cuts:
        heights = jnp.exp(jax.random.uniform(jax.random.fold_in(own, dim), (shards_of,), jnp.float32, smallest / len(cuts), high / len(cuts)))
        level = level * jnp.repeat(heights, shape[dim] // shards_of).reshape([-1 if axis == dim else 1 for axis in range(len(shape))])
    return level


def gaussian(key, extent, spread, reach, pieces=(), dtype=jnp.bfloat16):
    loudness = shard_levels(key, extent, pieces, -0.22, 0.18) if pieces else 1.0
    values = jax.random.normal(key, extent, jnp.float32) * spread * loudness
    return jnp.minimum(jnp.maximum(values, -reach), reach).astype(dtype)


def setup_inputs(seed: int = 0) -> dict:
    arg_keys = jax.random.split(jax.random.key(seed), 11)
    return {
        "fwd_input": draw_fwd_input(jax.random.fold_in(arg_keys[10], 71), 0),
        "saved_input": draw_saved_input(jax.random.fold_in(arg_keys[10], 71), 0),
        "out_grad": gaussian(arg_keys[2], (SECTIONS, BATCH, SEQ_LEN, D), 1.0, 6.0, ((0, 8), (1, 16), (2, 8))),
        "fwd_sky": touch_ends((jax.random.randint(arg_keys[3], (SECTIONS, BATCH, SEQ_LEN), 0, 4) < 1).astype(jnp.int32), jax.random.fold_in(arg_keys[3], 1), 0, 1),
        "bwd_sky": touch_ends((jax.random.randint(arg_keys[4], (SECTIONS, BATCH, SEQ_LEN), 0, 4) < 1).astype(jnp.int32), jax.random.fold_in(arg_keys[4], 1), 0, 1),
        "norm_gain": jnp.clip(1.0 + 0.1 * jax.random.normal(arg_keys[5], (SECTIONS, D), jnp.float32), 0.5, 1.5),
        "query_scale": draw_query_scale(jax.random.fold_in(arg_keys[10], 71), 0),
        "key_scale": draw_key_scale(jax.random.fold_in(arg_keys[10], 71), 0),
        "value_scale": gaussian(arg_keys[8], (SECTIONS, D), 1.0, 4.0, ((0, 8),), jnp.float32),
        "sky_bias": jnp.clip(-4.0 + 6.0 * jax.random.uniform(arg_keys[9], (SECTIONS, HEADS), jnp.float32) ** shard_levels(arg_keys[9], (SECTIONS, HEADS), ((0, 8),), -0.2, 0.2), -4.0, 2.0),
    }


epsilon = 1e-05

def project(rows, sum_squares, gains):
    norm_g, query_g, key_g, value_g = gains
    rows_f = rows.astype(jnp.float32)
    inv_root = lax.rsqrt(sum_squares[:, None] / D + epsilon)
    scaled = rows_f * inv_root
    normed = scaled * norm_g
    queries = (normed * query_g).astype(jnp.bfloat16)
    keys_low = (normed * key_g).astype(jnp.bfloat16)
    values_low = (normed * value_g).astype(jnp.bfloat16)
    return (scaled, normed, inv_root, queries, keys_low, values_low)

def window_of(rows, block):
    blocks = rows.reshape((8, block) + rows.shape[1:])
    previous = jnp.concatenate([jnp.zeros_like(blocks[:1]), blocks[:-1]], axis=0)
    return jnp.concatenate([previous, blocks], axis=1)

def fold_window(window_grads, block):
    later = window_grads[:, block:]
    earlier = jnp.concatenate([window_grads[1:, :block], jnp.zeros_like(window_grads[:1, :block])], axis=0)
    return later + earlier

def window_mask(block):
    inner = jnp.arange(block)[:, None]
    outer = jnp.arange(2 * block)[None, :]
    inside = (outer > inner) & (outer <= inner + block)
    first = jnp.arange(8)[:, None, None] > 0
    return inside[None] & (first | (outer >= block)[None])

def scores_of(query_blocks, key_window, head_bias, sky_window, block):
    factor = 1.0 / math.sqrt(HEAD_DIM)
    scores = jnp.einsum('bthd,buhd->bhtu', query_blocks, key_window) * factor
    scores = scores + head_bias[None, :, None, None] * sky_window[:, None, None, :]
    return jnp.where(window_mask(block)[:, None], scores, -1e+30)

def attend(query_rows, key_rows, value_rows, head_bias, sky_row):
    length, channels = query_rows.shape
    head_count = channels // HEAD_DIM
    block = length // 8
    query_blocks = query_rows.reshape(8, block, head_count, HEAD_DIM).astype(jnp.float32)
    key_window = window_of(key_rows.reshape(length, head_count, HEAD_DIM), block).astype(jnp.float32)
    value_window = window_of(value_rows.reshape(length, head_count, HEAD_DIM), block).astype(jnp.float32)
    sky_window = window_of(sky_row.astype(jnp.float32), block)
    scores = scores_of(query_blocks, key_window, head_bias, sky_window, block)
    probs_low = jax.nn.softmax(scores, axis=-1).astype(jnp.bfloat16)
    weighted = jnp.einsum('bhtu,buhd->bthd', probs_low.astype(jnp.float32), value_window)
    return weighted.astype(jnp.bfloat16).reshape(length, channels)

def attend_back(query_rows, key_rows, value_rows, upstream_rows, head_bias, sky_row):
    length, channels = query_rows.shape
    head_count = channels // HEAD_DIM
    block = length // 8
    factor = 1.0 / math.sqrt(HEAD_DIM)
    query_blocks = query_rows.reshape(8, block, head_count, HEAD_DIM).astype(jnp.float32)
    upstream_blocks = upstream_rows.reshape(8, block, head_count, HEAD_DIM).astype(jnp.float32)
    key_window = window_of(key_rows.reshape(length, head_count, HEAD_DIM), block).astype(jnp.float32)
    value_window = window_of(value_rows.reshape(length, head_count, HEAD_DIM), block).astype(jnp.float32)
    sky_window = window_of(sky_row.astype(jnp.float32), block)
    scores = scores_of(query_blocks, key_window, head_bias, sky_window, block)
    probs = jax.nn.softmax(scores, axis=-1)
    probs_low = probs.astype(jnp.bfloat16).astype(jnp.float32)
    value_part = jnp.einsum('bhtu,bthd->buhd', probs_low, upstream_blocks)
    prob_grad = jnp.einsum('bthd,buhd->bhtu', upstream_blocks, value_window)
    score_grad = probs * (prob_grad - lax.optimization_barrier(jnp.sum(probs * prob_grad, axis=-1, keepdims=True)))
    bias_part = lax.optimization_barrier(jnp.sum(score_grad * sky_window[:, None, None, :], axis=(0, 2, 3)))
    score_low = score_grad.astype(jnp.bfloat16).astype(jnp.float32)
    query_grad = jnp.einsum('bhtu,buhd->bthd', score_low, key_window) * factor
    key_part = jnp.einsum('bhtu,bthd->buhd', score_low, query_blocks) * factor
    query_low = query_grad.reshape(length, channels).astype(jnp.bfloat16)
    key_low = fold_window(key_part, block).reshape(length, channels).astype(jnp.bfloat16)
    value_low = fold_window(value_part, block).reshape(length, channels).astype(jnp.bfloat16)
    return (query_low, key_low, value_low, bias_part)

def tail_start(query_low, key_low, value_low, scaled, normed, gains):
    norm_g, query_g, key_g, value_g = gains
    query_f = query_low.astype(jnp.float32)
    key_f = key_low.astype(jnp.float32)
    value_f = value_low.astype(jnp.float32)
    normed_grad = query_f * query_g + key_f * key_g + value_f * value_g
    scaled_grad = normed_grad * norm_g
    partials = jnp.stack([lax.optimization_barrier(jnp.sum(normed_grad * scaled, axis=0)), lax.optimization_barrier(jnp.sum(query_f * normed, axis=0)), lax.optimization_barrier(jnp.sum(key_f * normed, axis=0)), lax.optimization_barrier(jnp.sum(value_f * normed, axis=0))])
    local_mix = lax.optimization_barrier(jnp.sum(scaled_grad * scaled, axis=-1))
    return (scaled_grad, partials, local_mix)

def finish(upstream, scaled_grad, scaled, inv_root, mix_sum):
    result = upstream.astype(jnp.float32) + inv_root * (scaled_grad - scaled * (mix_sum[:, None] / D))
    return result.astype(jnp.bfloat16)

def section_forward(rows, sky_row, gains, head_bias):
    rows_f = rows.astype(jnp.float32)
    scaled, normed, inv_root, queries, keys_low, values_low = project(rows, lax.optimization_barrier(jnp.sum(rows_f * rows_f, axis=-1)), gains)
    attended = attend(queries, keys_low, values_low, head_bias, sky_row)
    return (rows_f + attended.astype(jnp.float32)).astype(jnp.bfloat16)

def section_backward(rows, sky_row, upstream, gains, head_bias):
    rows_f = rows.astype(jnp.float32)
    scaled, normed, inv_root, queries, keys_low, values_low = project(rows, lax.optimization_barrier(jnp.sum(rows_f * rows_f, axis=-1)), gains)
    query_low, key_low, value_low, bias_part = attend_back(queries, keys_low, values_low, upstream, head_bias, sky_row)
    scaled_grad, partials, local_mix = tail_start(query_low, key_low, value_low, scaled, normed, gains)
    return (finish(upstream, scaled_grad, scaled, inv_root, local_mix), partials, bias_part)

def reference(fwd_input, saved_input, out_grad, fwd_sky, bwd_sky, norm_gain, query_scale, key_scale, value_scale, sky_bias):

    def forward_section(packed):
        rows_all, sky_all, norm_g, query_g, key_g, value_g, head_bias = packed
        gains = (norm_g, query_g, key_g, value_g)
        return lax.map(lambda item: section_forward(item[0], item[1], gains, head_bias), (rows_all, sky_all))

    def backward_section(packed):
        rows_all, sky_all, grads_all, norm_g, query_g, key_g, value_g, head_bias = packed
        gains = (norm_g, query_g, key_g, value_g)
        return lax.map(lambda item: section_backward(item[0], item[1], item[2], gains, head_bias), (rows_all, sky_all, grads_all))
    outputs = lax.map(forward_section, (fwd_input, fwd_sky, norm_gain, query_scale, key_scale, value_scale, sky_bias))
    input_grads, partials, bias_parts = lax.map(backward_section, (saved_input, bwd_sky, out_grad, norm_gain, query_scale, key_scale, value_scale, sky_bias))
    fwd_output = jnp.roll(outputs, 1, axis=0)
    bwd_output = jnp.roll(input_grads, -1, axis=0)
    scale_grads = lax.optimization_barrier(jnp.sum(partials, axis=1)) / BATCH
    bias_grad = lax.optimization_barrier(jnp.sum(bias_parts, axis=1)) / BATCH
    return (fwd_output, bwd_output, scale_grads, bias_grad)
```

```python
import functools
import math

import jax
import jax.numpy as jnp
from jax import lax
from jax.experimental import pallas as pl
from jax.experimental.pallas import tpu as pltpu
from jax.sharding import PartitionSpec as P

D = 2048
HEAD_DIM = 128
BATCH = 16
BLOCK = 128
WIDE = 256
CHUNKS = D // WIDE
AHEAD = 3

epsilon = 1e-05
factor = 1.0 / math.sqrt(HEAD_DIM)
f32 = jnp.float32
bf16 = jnp.bfloat16
MESH = pl.DeviceIdType.MESH


def dot(a, b, contract):
    return lax.dot_general(a, b, ((contract[:1], contract[1:]), ((), ())), preferred_element_type=f32)


def column_of(row):
    return jnp.transpose(jnp.broadcast_to(row, (BLOCK, BLOCK)))


def twice(square):
    return jnp.concatenate([square, square], axis=1)


def kernel(
    sizes,
    fx_ref, sx_ref, og_ref, fsky_ref, bsky_ref, ng_ref, qs_ref, ks_ref, vs_ref, bias_ref,
    fo_ref, bo_ref, sg_ref, bg_ref,
    sx, og, fx, halo, crecv, csend, bsend, fsend, grads,
    ng, qs, ks, vs, fsky, bsky,
    inv_s, inv_f, inv_sp, inv_fp, sky_s, sky_f, mask,
    stat_send, stat_recv, part_send, part_recv, xs, zs, zr,
    load_sem, x_send, x_recv, c_send, c_recv, stat_sem, p_send, p_recv,
    xs_send, xs_recv, z_send, z_recv, fo_send, fo_recv, bo_send, bo_recv,
):
    n_dp, n_pipe, n_seq = sizes
    me = lax.axis_index("seq")
    pipe = lax.axis_index("pipe")
    dp = lax.axis_index("dp")
    nxt, prv = lax.rem(me + 1, n_seq), lax.rem(me + n_seq - 1, n_seq)
    pnext, pprev = lax.rem(pipe + 1, n_pipe), lax.rem(pipe + n_pipe - 1, n_pipe)
    zi, xi = dp // 4, lax.rem(dp, 4)
    x_peers = [zi * 4 + lax.rem(xi + d, 4) for d in (1, 2, 3)]
    z_peers = [(zi + 1 - 2 * lax.rem(zi, 2)) * 4 + xi, (3 - zi) * 4 + xi]

    barrier = pltpu.get_barrier_semaphore()
    greeted = [{"seq": lax.rem(me + d, n_seq)} for d in range(1, n_seq)]
    greeted += [{"pipe": pnext}, {"pipe": pprev}]
    if n_dp == 16:
        greeted += [{"dp": peer} for peer in x_peers + z_peers]
    for peer in greeted:
        pl.semaphore_signal(barrier, inc=1, device_id=peer, device_id_type=MESH)

    def columns(c):
        return pl.ds(pl.multiple_of(c * WIDE, WIDE), WIDE)

    loads = []
    for source, target in ((sx_ref, sx), (fx_ref, fx), (og_ref, og)):
        for c in range(CHUNKS):
            loads.append((source.at[:, c * WIDE : (c + 1) * WIDE], target.at[c]))
    for source, target in (
        (ng_ref, ng), (qs_ref, qs), (ks_ref, ks), (vs_ref, vs), (fsky_ref, fsky), (bsky_ref, bsky),
    ):
        loads.append((source, target))
    copies = [pltpu.make_async_copy(a, b, load_sem.at[i]) for i, (a, b) in enumerate(loads)]
    for copy in copies:
        copy.start()

    def halo_copy(source, c, slot):
        return pltpu.make_async_remote_copy(
            src_ref=source.at[:, columns(c)],
            dst_ref=halo.at[slot],
            send_sem=x_send.at[slot],
            recv_sem=x_recv.at[slot],
            device_id={"seq": nxt},
            device_id_type=MESH,
        )

    def saved_halo(c):
        return halo_copy(sx_ref, c, c)

    def forward_halo(c):
        return halo_copy(fx_ref, c, c + CHUNKS)

    pl.semaphore_wait(barrier, len(greeted))
    for c in range(AHEAD - 1):
        saved_halo(c).start()

    def inverse_root(target):
        def add(c, total):
            rows = target[c].astype(f32)
            return total + rows * rows

        total = lax.fori_loop(0, CHUNKS, add, jnp.zeros((BLOCK, WIDE), f32))
        return lax.rsqrt(jnp.sum(total, axis=1, keepdims=True) / D + epsilon)

    for copy in copies[:CHUNKS]:
        copy.wait()
    inv = jnp.broadcast_to(inverse_root(sx), (BLOCK, BLOCK))
    inv_s[...] = twice(inv)
    stat_send[0:4, :] = jnp.transpose(inv)[0:4, :]
    for copy in copies[CHUNKS : 2 * CHUNKS]:
        copy.wait()
    inv = jnp.broadcast_to(inverse_root(fx), (BLOCK, BLOCK))
    inv_f[...] = twice(inv)
    stat_send[4:8, :] = jnp.transpose(inv)[0:4, :]
    stat_copy = pltpu.make_async_remote_copy(
        src_ref=stat_send,
        dst_ref=stat_recv,
        send_sem=stat_sem.at[0],
        recv_sem=stat_sem.at[1],
        device_id={"seq": nxt},
        device_id_type=MESH,
    )
    stat_copy.start()
    saved_halo(AHEAD - 1).start()

    for copy in copies[2 * CHUNKS :]:
        copy.wait()

    for source, target in ((bsky, sky_s), (fsky, sky_f)):
        for half, block in ((0, prv), (1, me)):
            row = source[:, pl.ds(pl.multiple_of(block * BLOCK, BLOCK), BLOCK)].astype(f32)
            target[half * BLOCK : (half + 1) * BLOCK, :] = column_of(row)
    outer = lax.broadcasted_iota(jnp.int32, (2 * BLOCK, BLOCK), 0)
    inner = lax.broadcasted_iota(jnp.int32, (2 * BLOCK, BLOCK), 1)
    first_key = jnp.where(me > 0, 0, BLOCK)
    inside = (outer > inner) & (outer <= inner + BLOCK) & (outer >= first_key)
    mask[...] = jnp.where(inside, 0.0, -1e30).astype(f32)

    stat_copy.wait_recv()
    inv_sp[...] = twice(column_of(stat_recv[0:1, :]))
    inv_fp[...] = twice(column_of(stat_recv[4:5, :]))

    def gains_of(c):
        return tuple(r[:, columns(c)] for r in (ng, qs, ks, vs))

    def probabilities(key_window, query, head, sky):
        scores = dot(key_window, query, (1, 1)) * factor
        scores = scores + (bias_ref[0, head] * sky[...] + mask[...])
        top = jnp.max(scores, axis=0, keepdims=True)
        raised = jnp.exp(scores - top)
        return raised * (1.0 / jnp.sum(raised, axis=0, keepdims=True))

    def part_copy(c, slot, peer):
        return pltpu.make_async_remote_copy(
            src_ref=part_send.at[c],
            dst_ref=part_recv.at[slot],
            send_sem=p_send.at[c],
            recv_sem=p_recv.at[slot],
            device_id={"seq": peer},
            device_id_type=MESH,
        )

    def fold_copy(c):
        return pltpu.make_async_remote_copy(
            src_ref=csend.at[c],
            dst_ref=crecv.at[c],
            send_sem=c_send.at[c],
            recv_sem=c_recv.at[c],
            device_id={"seq": prv},
            device_id_type=MESH,
        )

    def backward_chunk(c, carry):
        saved_halo(c).wait_recv()
        gain, query_s, key_s, value_s = gains_of(c)
        scaled = sx[c].astype(f32) * inv_s[...]
        normed = scaled * gain
        query = (normed * query_s).astype(bf16)
        key = (normed * key_s).astype(bf16)
        value = (normed * value_s).astype(bf16)
        scaled_p = halo[c].astype(f32) * inv_sp[...]
        normed_p = scaled_p * gain
        key_p = (normed_p * key_s).astype(bf16)
        value_p = (normed_p * value_s).astype(bf16)
        upstream = og[c]
        query_grads, key_grads, value_grads, biases = [], [], [], []
        for h in range(2):
            s = slice(h * HEAD_DIM, (h + 1) * HEAD_DIM)
            query_h, upstream_h = query[:, s], upstream[:, s]
            key_window = jnp.concatenate([key_p[:, s], key[:, s]], axis=0)
            value_window = jnp.concatenate([value_p[:, s], value[:, s]], axis=0)
            probs = probabilities(key_window, query_h, 2 * c + h, sky_s)
            value_grads.append(dot(probs.astype(bf16), upstream_h, (1, 0)))
            prob_grad = dot(value_window, upstream_h, (1, 1))
            score_grad = probs * (prob_grad - jnp.sum(probs * prob_grad, axis=0, keepdims=True))
            biases.append(jnp.sum(score_grad * sky_s[...], axis=0, keepdims=True))
            score_low = score_grad.astype(bf16)
            key_grads.append(dot(score_low, query_h, (1, 0)) * factor)
            query_grads.append(dot(score_low, key_window, (0, 0)) * factor)
        query_grad = jnp.concatenate(query_grads, axis=1).astype(bf16).astype(f32)
        key_grad = jnp.concatenate(key_grads, axis=1)
        value_grad = jnp.concatenate(value_grads, axis=1)
        key_b, key_a = key_grad[:BLOCK], key_grad[BLOCK:]
        value_b, value_a = value_grad[:BLOCK], value_grad[BLOCK:]
        csend[c] = (key_b * key_s + value_b * value_s).astype(bf16)
        fold_copy(c).start()
        grads[c] = query_grad * query_s + key_a * key_s + value_a * value_s
        sums = (
            jnp.sum(query_grad * scaled, axis=0, keepdims=True),
            jnp.sum(key_a * scaled + key_b * scaled_p, axis=0, keepdims=True),
            jnp.sum(value_a * scaled + value_b * scaled_p, axis=0, keepdims=True),
        )
        for i, row in enumerate(sums):
            part_send[c, 2 * i : 2 * i + 1, :] = row[:, :HEAD_DIM]
            part_send[c, 2 * i + 1 : 2 * i + 2, :] = row[:, HEAD_DIM:]
        part_send[c, 6:7, :] = biases[0]
        part_send[c, 7:8, :] = biases[1]

        @pl.when(c != me)
        def _():
            part_copy(c, me, c).start()

        @pl.when(c < CHUNKS - AHEAD)
        def _():
            saved_halo(c + AHEAD).start()

        @pl.when(c >= CHUNKS - AHEAD)
        def _():
            forward_halo(c + AHEAD - CHUNKS).start()

        return carry

    lax.fori_loop(0, CHUNKS, backward_chunk, 0)

    def start_forward_halo(c, carry):
        forward_halo(c).start()
        return carry

    lax.fori_loop(AHEAD, CHUNKS, start_forward_halo, 0)

    def fold(c, total):
        fold_copy(c).wait_recv()
        scaled_grad = (grads[c] + crecv[c].astype(f32)) * ng[:, columns(c)]
        grads[c] = scaled_grad
        return total + scaled_grad * (sx[c].astype(f32) * inv_s[...])

    total = lax.fori_loop(0, CHUNKS, fold, jnp.zeros((BLOCK, WIDE), f32))
    mean = jnp.broadcast_to(jnp.sum(total, axis=1, keepdims=True) / D, (BLOCK, WIDE))

    def bwd_copy(c):
        return pltpu.make_async_remote_copy(
            src_ref=bsend.at[c],
            dst_ref=bo_ref.at[:, columns(c)],
            send_sem=bo_send.at[c],
            recv_sem=bo_recv.at[c],
            device_id={"pipe": pprev},
            device_id_type=MESH,
        )

    def finish(c, carry):
        root = inv_s[...]
        scaled = sx[c].astype(f32) * root
        bsend[c] = (og[c].astype(f32) + root * (grads[c] - scaled * carry)).astype(bf16)
        bwd_copy(c).start()
        return carry

    lax.fori_loop(0, CHUNKS, finish, mean)

    def fwd_copy(c):
        return pltpu.make_async_remote_copy(
            src_ref=fsend.at[c],
            dst_ref=fo_ref.at[:, columns(c)],
            send_sem=fo_send.at[c],
            recv_sem=fo_recv.at[c],
            device_id={"pipe": pnext},
            device_id_type=MESH,
        )

    def forward_chunk(c, carry):
        forward_halo(c).wait_recv()
        gain, query_s, key_s, value_s = gains_of(c)
        rows = fx[c].astype(f32)
        normed = rows * inv_f[...] * gain
        query = (normed * query_s).astype(bf16)
        key = (normed * key_s).astype(bf16)
        value = (normed * value_s).astype(bf16)
        normed_p = halo[c + CHUNKS].astype(f32) * inv_fp[...] * gain
        key_p = (normed_p * key_s).astype(bf16)
        value_p = (normed_p * value_s).astype(bf16)
        attended = []
        for h in range(2):
            s = slice(h * HEAD_DIM, (h + 1) * HEAD_DIM)
            key_window = jnp.concatenate([key_p[:, s], key[:, s]], axis=0)
            value_window = jnp.concatenate([value_p[:, s], value[:, s]], axis=0)
            probs = probabilities(key_window, query[:, s], 2 * c + h, sky_f).astype(bf16)
            attended.append(dot(probs, value_window, (0, 0)))
        attended = jnp.concatenate(attended, axis=1).astype(bf16).astype(f32)
        fsend[c] = (rows + attended).astype(bf16)
        fwd_copy(c).start()
        return carry

    def seq_sum():
        total = part_send[me]
        for d in range(1, n_seq):
            peer = lax.rem(me + d, n_seq)
            part_copy(peer, peer, peer).wait_recv()
            total = total + part_recv[peer]
        return total

    def x_copy(i):
        return pltpu.make_async_remote_copy(
            src_ref=xs.at[xi],
            dst_ref=xs.at[xi],
            send_sem=xs_send.at[i],
            recv_sem=xs_recv.at[xi],
            device_id={"dp": x_peers[i]},
            device_id_type=MESH,
        )

    def x_arrival(i):
        slot = lax.rem(xi + i + 1, 4)
        return pltpu.make_async_remote_copy(
            src_ref=xs.at[slot],
            dst_ref=xs.at[slot],
            send_sem=xs_send.at[i],
            recv_sem=xs_recv.at[slot],
            device_id={"dp": x_peers[i]},
            device_id_type=MESH,
        )

    def z_copy(i):
        return pltpu.make_async_remote_copy(
            src_ref=zs.at[i],
            dst_ref=zr.at[i],
            send_sem=z_send.at[i],
            recv_sem=z_recv.at[i],
            device_id={"dp": z_peers[i]},
            device_id_type=MESH,
        )

    lax.fori_loop(0, 3, forward_chunk, 0)
    total = seq_sum()
    if n_dp == 16:
        xs[xi] = total
        for i in range(3):
            x_copy(i).start()
    lax.fori_loop(3, 5, forward_chunk, 0)
    if n_dp == 16:
        for i in range(3):
            x_arrival(i).wait_recv()
        zs[0] = (xs[0] + xs[1]) + (xs[2] + xs[3])
        z_copy(0).start()
    lax.fori_loop(5, CHUNKS - 1, forward_chunk, 0)
    if n_dp == 16:
        z_copy(0).wait_recv()
        zs[1] = zs[0] + zr[0]
        z_copy(1).start()
    lax.fori_loop(CHUNKS - 1, CHUNKS, forward_chunk, 0)
    if n_dp == 16:
        z_copy(1).wait_recv()
        total = zs[1] + zr[1]

    total = total * (1.0 / BATCH)
    gain, query_s, key_s, value_s = gains_of(me)
    for h in range(2):
        s = slice(h * HEAD_DIM, (h + 1) * HEAD_DIM)
        query_sum, key_sum, value_sum = (total[2 * i + h : 2 * i + h + 1, :] for i in range(3))
        sg_ref[0:1, s] = query_sum * query_s[:, s] + key_sum * key_s[:, s] + value_sum * value_s[:, s]
        sg_ref[1:2, s] = query_sum * gain[:, s]
        sg_ref[2:3, s] = key_sum * gain[:, s]
        sg_ref[3:4, s] = value_sum * gain[:, s]
        bg_ref[0:1, h : h + 1] = jnp.sum(total[6 + h : 7 + h, :], axis=1, keepdims=True)

    stat_copy.wait_send()
    if n_dp == 16:
        for i in range(3):
            x_copy(i).wait_send()
        for i in range(2):
            z_copy(i).wait_send()
    for d in range(1, n_seq):
        peer = lax.rem(me + d, n_seq)
        part_copy(peer, peer, peer).wait_send()

    def drain(c, carry):
        saved_halo(c).wait_send()
        forward_halo(c).wait_send()
        fold_copy(c).wait_send()
        bwd_copy(c).wait()
        fwd_copy(c).wait()
        return carry

    lax.fori_loop(0, CHUNKS, drain, 0)


def solution(mesh):
    sizes = tuple(mesh.shape[name] for name in ("dp", "pipe", "seq"))
    rows = (BLOCK, D)

    def on_device(fwd_input, saved_input, out_grad, fwd_sky, bwd_sky, norm_gain, query_scale, key_scale, value_scale, sky_bias):
        hbm = pl.BlockSpec(memory_space=pltpu.MemorySpace.HBM)
        vmem = pl.BlockSpec(memory_space=pltpu.MemorySpace.VMEM)
        smem = pl.BlockSpec(memory_space=pltpu.MemorySpace.SMEM)
        chunked = pltpu.VMEM((CHUNKS, BLOCK, WIDE), bf16)
        wide = pltpu.VMEM((BLOCK, WIDE), f32)
        window = pltpu.VMEM((2 * BLOCK, BLOCK), f32)
        tile = (8, 128)
        sem = pltpu.SemaphoreType.DMA
        fo, bo, sg, bg = pl.pallas_call(
            functools.partial(kernel, sizes),
            out_shape=(
                jax.ShapeDtypeStruct(rows, bf16),
                jax.ShapeDtypeStruct(rows, bf16),
                jax.ShapeDtypeStruct((4, WIDE), f32),
                jax.ShapeDtypeStruct((1, 2), f32),
            ),
            in_specs=[hbm] * 9 + [smem],
            out_specs=(hbm, hbm, vmem, vmem),
            scratch_shapes=[
                chunked, chunked, chunked,
                pltpu.VMEM((2 * CHUNKS, BLOCK, WIDE), bf16),
                chunked, chunked, chunked, chunked,
                pltpu.VMEM((CHUNKS, BLOCK, WIDE), f32),
                pltpu.VMEM((1, D), f32), pltpu.VMEM((1, D), f32), pltpu.VMEM((1, D), f32), pltpu.VMEM((1, D), f32),
                pltpu.VMEM((1, D // 2), jnp.int32), pltpu.VMEM((1, D // 2), jnp.int32),
                wide, wide, wide, wide, window, window, window,
                pltpu.VMEM(tile, f32), pltpu.VMEM(tile, f32),
                pltpu.VMEM((CHUNKS,) + tile, f32), pltpu.VMEM((CHUNKS,) + tile, f32),
                pltpu.VMEM((4,) + tile, f32), pltpu.VMEM((2,) + tile, f32), pltpu.VMEM((2,) + tile, f32),
                sem((3 * CHUNKS + 6,)), sem((2 * CHUNKS,)), sem((2 * CHUNKS,)), sem((CHUNKS,)), sem((CHUNKS,)),
                sem((2,)), sem((CHUNKS,)), sem((CHUNKS,)),
                sem((3,)), sem((4,)), sem((2,)), sem((2,)),
                sem((CHUNKS,)), sem((CHUNKS,)), sem((CHUNKS,)), sem((CHUNKS,)),
            ],
            compiler_params=pltpu.CompilerParams(collective_id=0, has_side_effects=True),
            name="relay_tick",
        )(
            fwd_input.reshape(rows), saved_input.reshape(rows), out_grad.reshape(rows),
            fwd_sky.reshape(1, -1), bwd_sky.reshape(1, -1),
            norm_gain, query_scale, key_scale, value_scale, sky_bias,
        )
        return fo[None, None], bo[None, None], sg[None], bg

    placed = (
        P("pipe", "dp", "seq", None),
        P("pipe", "dp", "seq", None),
        P("pipe", "dp", "seq", None),
        P("pipe", "dp", None),
        P("pipe", "dp", None),
        P("pipe", None),
        P("pipe", None),
        P("pipe", None),
        P("pipe", None),
        P("pipe", None),
    )
    return jax.shard_map(
        on_device,
        mesh=mesh,
        in_specs=placed,
        out_specs=(
            P("pipe", "dp", "seq", None),
            P("pipe", "dp", "seq", None),
            P("pipe", None, "seq"),
            P("pipe", "seq"),
        ),
        check_vma=False,
    )
```

```python
import functools
import math

import jax
import jax.numpy as jnp
from jax import lax
from jax.experimental import pallas as pl
from jax.experimental.pallas import tpu as pltpu
from jax.sharding import PartitionSpec as P

D = 2048
HEAD_DIM = 128
BATCH = 16
BLOCK = 128
WIDE = 256
CHUNKS = D // WIDE
AHEAD = 2

epsilon = 1e-05
factor = 1.0 / math.sqrt(HEAD_DIM)
f32 = jnp.float32
bf16 = jnp.bfloat16
MESH = pl.DeviceIdType.MESH


def dot(a, b, contract):
    return lax.dot_general(a, b, ((contract[:1], contract[1:]), ((), ())), preferred_element_type=f32)


def column_of(row):
    return jnp.transpose(jnp.broadcast_to(row, (BLOCK, BLOCK)))


def twice(square):
    return jnp.concatenate([square, square], axis=1)


def kernel(
    sizes,
    fx_ref, sx_ref, og_ref, fsky_ref, bsky_ref, ng_ref, qs_ref, ks_ref, vs_ref, bias_ref,
    fo_ref, bo_ref, sg_ref, bg_ref,
    sx, og, fx, halo, crecv, csend, bsend, fsend, grads,
    ng, qs, ks, vs, fsky, bsky,
    inv_s, inv_f, inv_sp, inv_fp, sky_s, sky_f, mask,
    stat_send, stat_recv, part_send, part_recv, xs, zs,
    load_sem, x_send, x_recv, c_send, c_recv, stat_sem, p_send, p_recv,
    xs_send, xs_recv, z_send, z_recv, fo_send, fo_recv, bo_send, bo_recv, hello,
):
    n_dp, n_pipe, n_seq = sizes
    me = lax.axis_index("seq")
    pipe = lax.axis_index("pipe")
    dp = lax.axis_index("dp")
    nxt, prv = lax.rem(me + 1, n_seq), lax.rem(me + n_seq - 1, n_seq)
    pnext, pprev = lax.rem(pipe + 1, n_pipe), lax.rem(pipe + n_pipe - 1, n_pipe)
    zi, xi = dp // 4, lax.rem(dp, 4)

    def ring_rank(i, n):
        return jnp.minimum(i, n - i) * n + i

    groups = [[], [], [], []]
    for d in range(2, n_seq - 1):
        peer = lax.rem(me + d, n_seq)
        groups[0].append((ring_rank(peer, n_seq), ring_rank(me, n_seq), {"seq": peer}))
    if n_dp == 16:
        for d in (1, 2, 3):
            peer = lax.rem(xi + d, 4)
            groups[1].append((ring_rank(peer, 4), ring_rank(xi, 4), {"dp": zi * 4 + peer}))
            peer = lax.rem(zi + d, 4)
            groups[2].append((peer, zi, {"dp": peer * 4 + xi}))
    for peer in (pnext, pprev):
        groups[3].append((peer, pipe, {"pipe": peer}))

    barrier = pltpu.get_barrier_semaphore()
    for peer in (nxt, prv):
        pl.semaphore_signal(barrier, inc=1, device_id={"seq": peer}, device_id_type=MESH)
    elders = 2
    for group in groups:
        for rank, own, peer in group:
            elders = elders + jnp.where(rank < own, 1, 0)

            @pl.when(rank > own)
            def _():
                pl.semaphore_signal(barrier, inc=1, device_id=peer, device_id_type=MESH)

    def await_younger(i):
        younger = sum(jnp.where(rank > own, 1, 0) for rank, own, _ in groups[i])

        @pl.when(younger > 0)
        def _():
            pl.semaphore_wait(hello.at[i], younger)

    def columns(c):
        return pl.ds(pl.multiple_of(c * WIDE, WIDE), WIDE)

    loads = []
    for source, target in ((sx_ref, sx), (fx_ref, fx), (og_ref, og)):
        for c in range(CHUNKS):
            loads.append((source.at[:, c * WIDE : (c + 1) * WIDE], target.at[c]))
    for source, target in (
        (ng_ref, ng), (qs_ref, qs), (ks_ref, ks), (vs_ref, vs), (fsky_ref, fsky), (bsky_ref, bsky),
    ):
        loads.append((source, target))
    copies = [pltpu.make_async_copy(a, b, load_sem.at[i]) for i, (a, b) in enumerate(loads)]
    for copy in copies:
        copy.start()

    def halo_copy(source, c, slot):
        return pltpu.make_async_remote_copy(
            src_ref=source.at[:, columns(c)],
            dst_ref=halo.at[slot],
            send_sem=x_send.at[slot],
            recv_sem=x_recv.at[slot],
            device_id={"seq": nxt},
            device_id_type=MESH,
        )

    def saved_halo(c):
        return halo_copy(sx_ref, c, c)

    def forward_halo(c):
        return halo_copy(fx_ref, c, c + CHUNKS)

    pl.semaphore_wait(barrier, elders)
    for c in range(AHEAD):
        saved_halo(c).start()
    for i, group in enumerate(groups):
        for rank, own, peer in group:

            @pl.when(rank < own)
            def _():
                pl.semaphore_signal(hello.at[i], inc=1, device_id=peer, device_id_type=MESH)

    def inverse_root(target):
        def add(c, total):
            rows = target[c].astype(f32)
            return total + rows * rows

        total = lax.fori_loop(0, CHUNKS, add, jnp.zeros((BLOCK, WIDE), f32))
        return lax.rsqrt(jnp.sum(total, axis=1, keepdims=True) / D + epsilon)

    for copy in copies[:CHUNKS]:
        copy.wait()
    inv = jnp.broadcast_to(inverse_root(sx), (BLOCK, BLOCK))
    inv_s[...] = twice(inv)
    stat_send[0:4, :] = jnp.transpose(inv)[0:4, :]
    for copy in copies[CHUNKS : 2 * CHUNKS]:
        copy.wait()
    inv = jnp.broadcast_to(inverse_root(fx), (BLOCK, BLOCK))
    inv_f[...] = twice(inv)
    stat_send[4:8, :] = jnp.transpose(inv)[0:4, :]
    stat_copy = pltpu.make_async_remote_copy(
        src_ref=stat_send,
        dst_ref=stat_recv,
        send_sem=stat_sem.at[0],
        recv_sem=stat_sem.at[1],
        device_id={"seq": nxt},
        device_id_type=MESH,
    )
    stat_copy.start()
    for c in range(AHEAD, CHUNKS):
        saved_halo(c).start()

    for copy in copies[2 * CHUNKS :]:
        copy.wait()

    for source, target in ((bsky, sky_s), (fsky, sky_f)):
        for half, block in ((0, prv), (1, me)):
            row = source[:, pl.ds(pl.multiple_of(block * BLOCK, BLOCK), BLOCK)].astype(f32)
            target[half * BLOCK : (half + 1) * BLOCK, :] = column_of(row)
    outer = lax.broadcasted_iota(jnp.int32, (2 * BLOCK, BLOCK), 0)
    inner = lax.broadcasted_iota(jnp.int32, (2 * BLOCK, BLOCK), 1)
    first_key = jnp.where(me > 0, 0, BLOCK)
    inside = (outer > inner) & (outer <= inner + BLOCK) & (outer >= first_key)
    mask[...] = jnp.where(inside, 0.0, -1e30).astype(f32)

    stat_copy.wait_recv()
    inv_sp[...] = twice(column_of(stat_recv[0:1, :]))
    inv_fp[...] = twice(column_of(stat_recv[4:5, :]))

    def gains_of(c):
        return tuple(r[:, columns(c)] for r in (ng, qs, ks, vs))

    def probabilities(key_window, query, head, sky):
        scores = dot(key_window, query, (1, 1)) * factor
        scores = scores + (bias_ref[0, head] * sky[...] + mask[...])
        top = jnp.max(scores, axis=0, keepdims=True)
        raised = jnp.exp(scores - top)
        return raised * (1.0 / jnp.sum(raised, axis=0, keepdims=True))

    def part_copy(c, slot, peer):
        return pltpu.make_async_remote_copy(
            src_ref=part_send.at[c],
            dst_ref=part_recv.at[slot],
            send_sem=p_send.at[c],
            recv_sem=p_recv.at[slot],
            device_id={"seq": peer},
            device_id_type=MESH,
        )

    def fold_copy(c):
        return pltpu.make_async_remote_copy(
            src_ref=csend.at[c],
            dst_ref=crecv.at[c],
            send_sem=c_send.at[c],
            recv_sem=c_recv.at[c],
            device_id={"seq": prv},
            device_id_type=MESH,
        )

    def backward_chunk(c, carry):
        saved_halo(c).wait_recv()
        gain, query_s, key_s, value_s = gains_of(c)
        scaled = sx[c].astype(f32) * inv_s[...]
        normed = scaled * gain
        query = (normed * query_s).astype(bf16)
        key = (normed * key_s).astype(bf16)
        value = (normed * value_s).astype(bf16)
        scaled_p = halo[c].astype(f32) * inv_sp[...]
        normed_p = scaled_p * gain
        key_p = (normed_p * key_s).astype(bf16)
        value_p = (normed_p * value_s).astype(bf16)
        upstream = og[c]
        query_grads, key_grads, value_grads, biases = [], [], [], []
        for h in range(2):
            s = slice(h * HEAD_DIM, (h + 1) * HEAD_DIM)
            query_h, upstream_h = query[:, s], upstream[:, s]
            key_window = jnp.concatenate([key_p[:, s], key[:, s]], axis=0)
            value_window = jnp.concatenate([value_p[:, s], value[:, s]], axis=0)
            probs = probabilities(key_window, query_h, 2 * c + h, sky_s)
            value_grads.append(dot(probs.astype(bf16), upstream_h, (1, 0)))
            prob_grad = dot(value_window, upstream_h, (1, 1))
            score_grad = probs * (prob_grad - jnp.sum(probs * prob_grad, axis=0, keepdims=True))
            biases.append(jnp.sum(score_grad * sky_s[...], axis=0, keepdims=True))
            score_low = score_grad.astype(bf16)
            key_grads.append(dot(score_low, query_h, (1, 0)) * factor)
            query_grads.append(dot(score_low, key_window, (0, 0)) * factor)
        query_grad = jnp.concatenate(query_grads, axis=1).astype(bf16).astype(f32)
        key_grad = jnp.concatenate(key_grads, axis=1)
        value_grad = jnp.concatenate(value_grads, axis=1)
        key_b, key_a = key_grad[:BLOCK], key_grad[BLOCK:]
        value_b, value_a = value_grad[:BLOCK], value_grad[BLOCK:]
        csend[c] = (key_b * key_s + value_b * value_s).astype(bf16)
        fold_copy(c).start()
        grads[c] = query_grad * query_s + key_a * key_s + value_a * value_s
        sums = (
            jnp.sum(query_grad * scaled, axis=0, keepdims=True),
            jnp.sum(key_a * scaled + key_b * scaled_p, axis=0, keepdims=True),
            jnp.sum(value_a * scaled + value_b * scaled_p, axis=0, keepdims=True),
        )
        for i, row in enumerate(sums):
            part_send[c, 2 * i : 2 * i + 1, :] = row[:, :HEAD_DIM]
            part_send[c, 2 * i + 1 : 2 * i + 2, :] = row[:, HEAD_DIM:]
        part_send[c, 6:7, :] = biases[0]
        part_send[c, 7:8, :] = biases[1]

        @pl.when(c == 1)
        def _():
            await_younger(0)

        @pl.when((c == 1) & (me != 0))
        def _():
            part_copy(0, me, 0).start()

        @pl.when((c >= 1) & (c != me))
        def _():
            part_copy(c, me, c).start()

        return carry

    lax.fori_loop(0, CHUNKS, backward_chunk, 0)

    def fold(c, total):
        fold_copy(c).wait_recv()
        scaled_grad = (grads[c] + crecv[c].astype(f32)) * ng[:, columns(c)]
        grads[c] = scaled_grad
        return total + scaled_grad * (sx[c].astype(f32) * inv_s[...])

    def bwd_copy(c):
        return pltpu.make_async_remote_copy(
            src_ref=bsend.at[c],
            dst_ref=bo_ref.at[:, columns(c)],
            send_sem=bo_send.at[c],
            recv_sem=bo_recv.at[c],
            device_id={"pipe": pprev},
            device_id_type=MESH,
        )

    def finish(c, carry):
        root = inv_s[...]
        scaled = sx[c].astype(f32) * root
        bsend[c] = (og[c].astype(f32) + root * (grads[c] - scaled * carry)).astype(bf16)
        bwd_copy(c).start()
        return carry

    def fwd_copy(c):
        return pltpu.make_async_remote_copy(
            src_ref=fsend.at[c],
            dst_ref=fo_ref.at[:, columns(c)],
            send_sem=fo_send.at[c],
            recv_sem=fo_recv.at[c],
            device_id={"pipe": pnext},
            device_id_type=MESH,
        )

    def forward_chunk(c, carry):
        forward_halo(c).wait_recv()
        gain, query_s, key_s, value_s = gains_of(c)
        rows = fx[c].astype(f32)
        normed = rows * inv_f[...] * gain
        query = (normed * query_s).astype(bf16)
        key = (normed * key_s).astype(bf16)
        value = (normed * value_s).astype(bf16)
        normed_p = halo[c + CHUNKS].astype(f32) * inv_fp[...] * gain
        key_p = (normed_p * key_s).astype(bf16)
        value_p = (normed_p * value_s).astype(bf16)
        attended = []
        for h in range(2):
            s = slice(h * HEAD_DIM, (h + 1) * HEAD_DIM)
            key_window = jnp.concatenate([key_p[:, s], key[:, s]], axis=0)
            value_window = jnp.concatenate([value_p[:, s], value[:, s]], axis=0)
            probs = probabilities(key_window, query[:, s], 2 * c + h, sky_f).astype(bf16)
            attended.append(dot(probs, value_window, (0, 0)))
        attended = jnp.concatenate(attended, axis=1).astype(bf16).astype(f32)
        fsend[c] = (rows + attended).astype(bf16)
        fwd_copy(c).start()
        return carry

    def seq_sum():
        total = part_send[me]
        for d in range(1, n_seq):
            peer = lax.rem(me + d, n_seq)
            part_copy(peer, peer, peer).wait_recv()
            total = total + part_recv[peer]
        return total

    def x_copy(i):
        return pltpu.make_async_remote_copy(
            src_ref=xs.at[xi],
            dst_ref=xs.at[xi],
            send_sem=xs_send.at[i],
            recv_sem=xs_recv.at[xi],
            device_id=groups[1][i][2],
            device_id_type=MESH,
        )

    def x_arrival(i):
        slot = lax.rem(xi + i + 1, 4)
        return pltpu.make_async_remote_copy(
            src_ref=xs.at[slot],
            dst_ref=xs.at[slot],
            send_sem=xs_send.at[i],
            recv_sem=xs_recv.at[slot],
            device_id=groups[1][i][2],
            device_id_type=MESH,
        )

    def z_copy(i):
        return pltpu.make_async_remote_copy(
            src_ref=zs.at[zi],
            dst_ref=zs.at[zi],
            send_sem=z_send.at[i],
            recv_sem=z_recv.at[zi],
            device_id=groups[2][i][2],
            device_id_type=MESH,
        )

    def z_arrival(i):
        slot = lax.rem(zi + i + 1, 4)
        return pltpu.make_async_remote_copy(
            src_ref=zs.at[slot],
            dst_ref=zs.at[slot],
            send_sem=z_send.at[i],
            recv_sem=z_recv.at[slot],
            device_id=groups[2][i][2],
            device_id_type=MESH,
        )

    def z_start(to_elders):
        for i, (rank, own, _) in enumerate(groups[2]):

            @pl.when(rank < own if to_elders else rank > own)
            def _():
                z_copy(i).start()

    total = lax.fori_loop(0, CHUNKS, fold, jnp.zeros((BLOCK, WIDE), f32))
    mean = jnp.broadcast_to(jnp.sum(total, axis=1, keepdims=True) / D, (BLOCK, WIDE))

    total = seq_sum()
    if n_dp == 16:
        xs[xi] = total
        await_younger(1)
        for i in range(3):
            x_copy(i).start()
    for c in range(CHUNKS):
        forward_halo(c).start()
    if n_dp == 16:
        for i in range(3):
            x_arrival(i).wait_recv()
        zs[zi] = (xs[0] + xs[1]) + (xs[2] + xs[3])
        z_start(True)
    await_younger(3)
    lax.fori_loop(0, CHUNKS, finish, mean)
    lax.fori_loop(0, CHUNKS, forward_chunk, 0)
    if n_dp == 16:
        await_younger(2)
        z_start(False)
        for i in range(3):
            z_arrival(i).wait_recv()
        total = (zs[0] + zs[1]) + (zs[2] + zs[3])

    total = total * (1.0 / BATCH)
    gain, query_s, key_s, value_s = gains_of(me)
    for h in range(2):
        s = slice(h * HEAD_DIM, (h + 1) * HEAD_DIM)
        query_sum, key_sum, value_sum = (total[2 * i + h : 2 * i + h + 1, :] for i in range(3))
        sg_ref[0:1, s] = query_sum * query_s[:, s] + key_sum * key_s[:, s] + value_sum * value_s[:, s]
        sg_ref[1:2, s] = query_sum * gain[:, s]
        sg_ref[2:3, s] = key_sum * gain[:, s]
        sg_ref[3:4, s] = value_sum * gain[:, s]
        bg_ref[0:1, h : h + 1] = jnp.sum(total[6 + h : 7 + h, :], axis=1, keepdims=True)

    stat_copy.wait_send()
    if n_dp == 16:
        for i in range(3):
            x_copy(i).wait_send()
            z_copy(i).wait_send()
    for d in range(1, n_seq):
        peer = lax.rem(me + d, n_seq)
        part_copy(peer, peer, peer).wait_send()

    def drain(c, carry):
        saved_halo(c).wait_send()
        forward_halo(c).wait_send()
        fold_copy(c).wait_send()
        bwd_copy(c).wait()
        fwd_copy(c).wait()
        return carry

    lax.fori_loop(0, CHUNKS, drain, 0)


def solution(mesh):
    sizes = tuple(mesh.shape[name] for name in ("dp", "pipe", "seq"))
    rows = (BLOCK, D)

    def on_device(fwd_input, saved_input, out_grad, fwd_sky, bwd_sky, norm_gain, query_scale, key_scale, value_scale, sky_bias):
        hbm = pl.BlockSpec(memory_space=pltpu.MemorySpace.HBM)
        vmem = pl.BlockSpec(memory_space=pltpu.MemorySpace.VMEM)
        smem = pl.BlockSpec(memory_space=pltpu.MemorySpace.SMEM)
        chunked = pltpu.VMEM((CHUNKS, BLOCK, WIDE), bf16)
        wide = pltpu.VMEM((BLOCK, WIDE), f32)
        window = pltpu.VMEM((2 * BLOCK, BLOCK), f32)
        tile = (8, 128)
        sem = pltpu.SemaphoreType.DMA
        fo, bo, sg, bg = pl.pallas_call(
            functools.partial(kernel, sizes),
            out_shape=(
                jax.ShapeDtypeStruct(rows, bf16),
                jax.ShapeDtypeStruct(rows, bf16),
                jax.ShapeDtypeStruct((4, WIDE), f32),
                jax.ShapeDtypeStruct((1, 2), f32),
            ),
            in_specs=[hbm] * 9 + [smem],
            out_specs=(hbm, hbm, vmem, vmem),
            scratch_shapes=[
                chunked, chunked, chunked,
                pltpu.VMEM((2 * CHUNKS, BLOCK, WIDE), bf16),
                chunked, chunked, chunked, chunked,
                pltpu.VMEM((CHUNKS, BLOCK, WIDE), f32),
                pltpu.VMEM((1, D), f32), pltpu.VMEM((1, D), f32), pltpu.VMEM((1, D), f32), pltpu.VMEM((1, D), f32),
                pltpu.VMEM((1, D // 2), jnp.int32), pltpu.VMEM((1, D // 2), jnp.int32),
                wide, wide, wide, wide, window, window, window,
                pltpu.VMEM(tile, f32), pltpu.VMEM(tile, f32),
                pltpu.VMEM((CHUNKS,) + tile, f32), pltpu.VMEM((CHUNKS,) + tile, f32),
                pltpu.VMEM((4,) + tile, f32), pltpu.VMEM((4,) + tile, f32),
                sem((3 * CHUNKS + 6,)), sem((2 * CHUNKS,)), sem((2 * CHUNKS,)), sem((CHUNKS,)), sem((CHUNKS,)),
                sem((2,)), sem((CHUNKS,)), sem((CHUNKS,)),
                sem((3,)), sem((4,)), sem((3,)), sem((4,)),
                sem((CHUNKS,)), sem((CHUNKS,)), sem((CHUNKS,)), sem((CHUNKS,)),
                pltpu.SemaphoreType.REGULAR((4,)),
            ],
            compiler_params=pltpu.CompilerParams(collective_id=0, has_side_effects=True),
            name="relay_tick",
        )(
            fwd_input.reshape(rows), saved_input.reshape(rows), out_grad.reshape(rows),
            fwd_sky.reshape(1, -1), bwd_sky.reshape(1, -1),
            norm_gain, query_scale, key_scale, value_scale, sky_bias,
        )
        return fo[None, None], bo[None, None], sg[None], bg

    placed = (
        P("pipe", "dp", "seq", None),
        P("pipe", "dp", "seq", None),
        P("pipe", "dp", "seq", None),
        P("pipe", "dp", None),
        P("pipe", "dp", None),
        P("pipe", None),
        P("pipe", None),
        P("pipe", None),
        P("pipe", None),
        P("pipe", None),
    )
    return jax.shard_map(
        on_device,
        mesh=mesh,
        in_specs=placed,
        out_specs=(
            P("pipe", "dp", "seq", None),
            P("pipe", "dp", "seq", None),
            P("pipe", None, "seq"),
            P("pipe", "seq"),
        ),
        check_vma=False,
    )
```

```python
import functools
import math

import jax
import jax.numpy as jnp
from jax import lax
from jax.experimental import pallas as pl
from jax.experimental.pallas import tpu as pltpu
from jax.sharding import PartitionSpec as P

D = 2048
HEAD_DIM = 128
BATCH = 16
BLOCK = 128
WIDE = 256
CHUNKS = D // WIDE
AHEAD = 2

epsilon = 1e-05
factor = 1.0 / math.sqrt(HEAD_DIM)
f32 = jnp.float32
bf16 = jnp.bfloat16
MESH = pl.DeviceIdType.MESH


def dot(a, b, contract):
    return lax.dot_general(a, b, ((contract[:1], contract[1:]), ((), ())), preferred_element_type=f32)


def column_of(row):
    return jnp.transpose(jnp.broadcast_to(row, (BLOCK, BLOCK)))


def turn(i, at):
    if isinstance(i, int):
        return lax.rem(at + (2 * (i % 2) - 1) * ((CHUNKS - i) // 2) + CHUNKS, CHUNKS)
    return lax.rem(at + (2 * lax.rem(i, 2) - 1) * lax.div(CHUNKS - i, 2) + CHUNKS, CHUNKS)


def twice(square):
    return jnp.concatenate([square, square], axis=1)


def kernel(
    sizes,
    fx_ref, sx_ref, og_ref, fsky_ref, bsky_ref, ng_ref, qs_ref, ks_ref, vs_ref, bias_ref,
    fo_ref, bo_ref, sg_ref, bg_ref,
    sx, og, fx, halo, crecv, csend, bsend, fsend, grads,
    ng, qs, ks, vs, fsky, bsky,
    inv_s, inv_f, inv_sp, inv_fp, sky_s, sky_f, mask,
    stat_send, stat_recv, part_send, part_recv, xs, zs,
    load_sem, x_send, x_recv, c_send, c_recv, stat_sem, p_send, p_recv,
    xs_send, xs_recv, z_send, z_recv, fo_send, fo_recv, bo_send, bo_recv, hello,
):
    n_dp, n_pipe, n_seq = sizes
    me = lax.axis_index("seq")
    pipe = lax.axis_index("pipe")
    dp = lax.axis_index("dp")
    nxt, prv = lax.rem(me + 1, n_seq), lax.rem(me + n_seq - 1, n_seq)
    pnext, pprev = lax.rem(pipe + 1, n_pipe), lax.rem(pipe + n_pipe - 1, n_pipe)
    zi, xi = dp // 4, lax.rem(dp, 4)

    def ring_rank(i, n):
        return jnp.minimum(i, n - i) * n + i

    groups = [[], [], [], []]
    for d in range(2, n_seq - 1):
        peer = lax.rem(me + d, n_seq)
        groups[0].append((ring_rank(peer, n_seq), ring_rank(me, n_seq), {"seq": peer}))
    if n_dp == 16:
        for d in (1, 2, 3):
            peer = lax.rem(xi + d, 4)
            groups[1].append((ring_rank(peer, 4), ring_rank(xi, 4), {"dp": zi * 4 + peer}))
            peer = lax.rem(zi + d, 4)
            groups[2].append((peer, zi, {"dp": peer * 4 + xi}))
    for peer in (pnext, pprev):
        groups[3].append((peer, pipe, {"pipe": peer}))

    barrier = pltpu.get_barrier_semaphore()
    for peer in (nxt, prv):
        pl.semaphore_signal(barrier, inc=1, device_id={"seq": peer}, device_id_type=MESH)
    elders = 2
    for group in groups:
        for rank, own, peer in group:
            elders = elders + jnp.where(rank < own, 1, 0)

            @pl.when(rank > own)
            def _():
                pl.semaphore_signal(barrier, inc=1, device_id=peer, device_id_type=MESH)

    def await_younger(i):
        younger = sum(jnp.where(rank > own, 1, 0) for rank, own, _ in groups[i])

        @pl.when(younger > 0)
        def _():
            pl.semaphore_wait(hello.at[i], younger)

    def columns(c):
        return pl.ds(pl.multiple_of(c * WIDE, WIDE), WIDE)

    loads = []
    for source, target in ((sx_ref, sx), (fx_ref, fx), (og_ref, og)):
        for c in range(CHUNKS):
            loads.append((source.at[:, c * WIDE : (c + 1) * WIDE], target.at[c]))
    for source, target in (
        (ng_ref, ng), (qs_ref, qs), (ks_ref, ks), (vs_ref, vs), (fsky_ref, fsky), (bsky_ref, bsky),
    ):
        loads.append((source, target))
    copies = [pltpu.make_async_copy(a, b, load_sem.at[i]) for i, (a, b) in enumerate(loads)]
    for copy in copies:
        copy.start()

    def halo_copy(source, c, slot):
        return pltpu.make_async_remote_copy(
            src_ref=source.at[:, columns(c)],
            dst_ref=halo.at[slot],
            send_sem=x_send.at[slot],
            recv_sem=x_recv.at[slot],
            device_id={"seq": nxt},
            device_id_type=MESH,
        )

    def saved_halo(c):
        return halo_copy(sx_ref, c, c)

    def forward_halo(c):
        return halo_copy(fx_ref, c, c + CHUNKS)

    pl.semaphore_wait(barrier, elders)
    for i in range(AHEAD):
        saved_halo(turn(i, nxt)).start()
    for i, group in enumerate(groups):
        for rank, own, peer in group:

            @pl.when(rank < own)
            def _():
                pl.semaphore_signal(hello.at[i], inc=1, device_id=peer, device_id_type=MESH)

    def inverse_root(target):
        def add(c, total):
            rows = target[c].astype(f32)
            return total + rows * rows

        total = lax.fori_loop(0, CHUNKS, add, jnp.zeros((BLOCK, WIDE), f32))
        return lax.rsqrt(jnp.sum(total, axis=1, keepdims=True) / D + epsilon)

    for copy in copies[:CHUNKS]:
        copy.wait()
    inv = jnp.broadcast_to(inverse_root(sx), (BLOCK, BLOCK))
    inv_s[...] = twice(inv)
    stat_send[0:4, :] = jnp.transpose(inv)[0:4, :]
    for copy in copies[CHUNKS : 2 * CHUNKS]:
        copy.wait()
    inv = jnp.broadcast_to(inverse_root(fx), (BLOCK, BLOCK))
    inv_f[...] = twice(inv)
    stat_send[4:8, :] = jnp.transpose(inv)[0:4, :]
    stat_copy = pltpu.make_async_remote_copy(
        src_ref=stat_send,
        dst_ref=stat_recv,
        send_sem=stat_sem.at[0],
        recv_sem=stat_sem.at[1],
        device_id={"seq": nxt},
        device_id_type=MESH,
    )
    stat_copy.start()
    for i in range(AHEAD, CHUNKS):
        saved_halo(turn(i, nxt)).start()

    for copy in copies[2 * CHUNKS :]:
        copy.wait()

    for source, target in ((bsky, sky_s), (fsky, sky_f)):
        for half, block in ((0, prv), (1, me)):
            row = source[:, pl.ds(pl.multiple_of(block * BLOCK, BLOCK), BLOCK)].astype(f32)
            target[half * BLOCK : (half + 1) * BLOCK, :] = column_of(row)
    outer = lax.broadcasted_iota(jnp.int32, (2 * BLOCK, BLOCK), 0)
    inner = lax.broadcasted_iota(jnp.int32, (2 * BLOCK, BLOCK), 1)
    first_key = jnp.where(me > 0, 0, BLOCK)
    inside = (outer > inner) & (outer <= inner + BLOCK) & (outer >= first_key)
    mask[...] = jnp.where(inside, 0.0, -1e30).astype(f32)

    stat_copy.wait_recv()
    inv_sp[...] = twice(column_of(stat_recv[0:1, :]))
    inv_fp[...] = twice(column_of(stat_recv[4:5, :]))

    def gains_of(c):
        return tuple(r[:, columns(c)] for r in (ng, qs, ks, vs))

    def probabilities(key_window, query, head, sky):
        scores = dot(key_window, query, (1, 1)) * factor
        scores = scores + (bias_ref[0, head] * sky[...] + mask[...])
        top = jnp.max(scores, axis=0, keepdims=True)
        raised = jnp.exp(scores - top)
        return raised * (1.0 / jnp.sum(raised, axis=0, keepdims=True))

    def part_copy(c, slot, peer):
        return pltpu.make_async_remote_copy(
            src_ref=part_send.at[c],
            dst_ref=part_recv.at[slot],
            send_sem=p_send.at[c],
            recv_sem=p_recv.at[slot],
            device_id={"seq": peer},
            device_id_type=MESH,
        )

    def fold_copy(c):
        return pltpu.make_async_remote_copy(
            src_ref=csend.at[c],
            dst_ref=crecv.at[c],
            send_sem=c_send.at[c],
            recv_sem=c_recv.at[c],
            device_id={"seq": prv},
            device_id_type=MESH,
        )

    def backward_chunk(i, carry):
        c = turn(i, me)
        saved_halo(c).wait_recv()
        gain, query_s, key_s, value_s = gains_of(c)
        scaled = sx[c].astype(f32) * inv_s[...]
        normed = scaled * gain
        query = (normed * query_s).astype(bf16)
        key = (normed * key_s).astype(bf16)
        value = (normed * value_s).astype(bf16)
        scaled_p = halo[c].astype(f32) * inv_sp[...]
        normed_p = scaled_p * gain
        key_p = (normed_p * key_s).astype(bf16)
        value_p = (normed_p * value_s).astype(bf16)
        upstream = og[c]
        query_grads, key_grads, value_grads, biases = [], [], [], []
        for h in range(2):
            s = slice(h * HEAD_DIM, (h + 1) * HEAD_DIM)
            query_h, upstream_h = query[:, s], upstream[:, s]
            key_window = jnp.concatenate([key_p[:, s], key[:, s]], axis=0)
            value_window = jnp.concatenate([value_p[:, s], value[:, s]], axis=0)
            probs = probabilities(key_window, query_h, 2 * c + h, sky_s)
            value_grads.append(dot(probs.astype(bf16), upstream_h, (1, 0)))
            prob_grad = dot(value_window, upstream_h, (1, 1))
            score_grad = probs * (prob_grad - jnp.sum(probs * prob_grad, axis=0, keepdims=True))
            biases.append(jnp.sum(score_grad * sky_s[...], axis=0, keepdims=True))
            score_low = score_grad.astype(bf16)
            key_grads.append(dot(score_low, query_h, (1, 0)) * factor)
            query_grads.append(dot(score_low, key_window, (0, 0)) * factor)
        query_grad = jnp.concatenate(query_grads, axis=1).astype(bf16).astype(f32)
        key_grad = jnp.concatenate(key_grads, axis=1)
        value_grad = jnp.concatenate(value_grads, axis=1)
        key_b, key_a = key_grad[:BLOCK], key_grad[BLOCK:]
        value_b, value_a = value_grad[:BLOCK], value_grad[BLOCK:]
        csend[c] = (key_b * key_s + value_b * value_s).astype(bf16)
        fold_copy(c).start()
        grads[c] = query_grad * query_s + key_a * key_s + value_a * value_s
        sums = (
            jnp.sum(query_grad * scaled, axis=0, keepdims=True),
            jnp.sum(key_a * scaled + key_b * scaled_p, axis=0, keepdims=True),
            jnp.sum(value_a * scaled + value_b * scaled_p, axis=0, keepdims=True),
        )
        for j, row in enumerate(sums):
            part_send[c, 2 * j : 2 * j + 1, :] = row[:, :HEAD_DIM]
            part_send[c, 2 * j + 1 : 2 * j + 2, :] = row[:, HEAD_DIM:]
        part_send[c, 6:7, :] = biases[0]
        part_send[c, 7:8, :] = biases[1]

        @pl.when(i == 1)
        def _():
            await_younger(0)
            first = turn(0, me)
            part_copy(first, me, first).start()

        @pl.when((i >= 1) & (i < CHUNKS - 1))
        def _():
            part_copy(c, me, c).start()

        return carry

    lax.fori_loop(0, CHUNKS, backward_chunk, 0)
    for c in range(CHUNKS):
        forward_halo(c).start()

    def fold(c, total):
        fold_copy(c).wait_recv()
        scaled_grad = (grads[c] + crecv[c].astype(f32)) * ng[:, columns(c)]
        grads[c] = scaled_grad
        return total + scaled_grad * (sx[c].astype(f32) * inv_s[...])

    def bwd_copy(c):
        return pltpu.make_async_remote_copy(
            src_ref=bsend.at[c],
            dst_ref=bo_ref.at[:, columns(c)],
            send_sem=bo_send.at[c],
            recv_sem=bo_recv.at[c],
            device_id={"pipe": pprev},
            device_id_type=MESH,
        )

    def finish(c, carry):
        root = inv_s[...]
        scaled = sx[c].astype(f32) * root
        bsend[c] = (og[c].astype(f32) + root * (grads[c] - scaled * carry)).astype(bf16)
        bwd_copy(c).start()
        return carry

    def fwd_copy(c):
        return pltpu.make_async_remote_copy(
            src_ref=fsend.at[c],
            dst_ref=fo_ref.at[:, columns(c)],
            send_sem=fo_send.at[c],
            recv_sem=fo_recv.at[c],
            device_id={"pipe": pnext},
            device_id_type=MESH,
        )

    def forward_chunk(c, carry):
        forward_halo(c).wait_recv()
        gain, query_s, key_s, value_s = gains_of(c)
        rows = fx[c].astype(f32)
        normed = rows * inv_f[...] * gain
        query = (normed * query_s).astype(bf16)
        key = (normed * key_s).astype(bf16)
        value = (normed * value_s).astype(bf16)
        normed_p = halo[c + CHUNKS].astype(f32) * inv_fp[...] * gain
        key_p = (normed_p * key_s).astype(bf16)
        value_p = (normed_p * value_s).astype(bf16)
        attended = []
        for h in range(2):
            s = slice(h * HEAD_DIM, (h + 1) * HEAD_DIM)
            key_window = jnp.concatenate([key_p[:, s], key[:, s]], axis=0)
            value_window = jnp.concatenate([value_p[:, s], value[:, s]], axis=0)
            probs = probabilities(key_window, query[:, s], 2 * c + h, sky_f).astype(bf16)
            attended.append(dot(probs, value_window, (0, 0)))
        attended = jnp.concatenate(attended, axis=1).astype(bf16).astype(f32)
        fsend[c] = (rows + attended).astype(bf16)
        fwd_copy(c).start()
        return carry

    def seq_sum():
        total = part_send[me]
        for d in range(1, n_seq):
            peer = lax.rem(me + d, n_seq)
            part_copy(peer, peer, peer).wait_recv()
            total = total + part_recv[peer]
        return total

    def x_copy(i):
        return pltpu.make_async_remote_copy(
            src_ref=xs.at[xi],
            dst_ref=xs.at[xi],
            send_sem=xs_send.at[i],
            recv_sem=xs_recv.at[xi],
            device_id=groups[1][i][2],
            device_id_type=MESH,
        )

    def x_arrival(i):
        slot = lax.rem(xi + i + 1, 4)
        return pltpu.make_async_remote_copy(
            src_ref=xs.at[slot],
            dst_ref=xs.at[slot],
            send_sem=xs_send.at[i],
            recv_sem=xs_recv.at[slot],
            device_id=groups[1][i][2],
            device_id_type=MESH,
        )

    def z_copy(i):
        return pltpu.make_async_remote_copy(
            src_ref=zs.at[zi],
            dst_ref=zs.at[zi],
            send_sem=z_send.at[i],
            recv_sem=z_recv.at[zi],
            device_id=groups[2][i][2],
            device_id_type=MESH,
        )

    def z_arrival(i):
        slot = lax.rem(zi + i + 1, 4)
        return pltpu.make_async_remote_copy(
            src_ref=zs.at[slot],
            dst_ref=zs.at[slot],
            send_sem=z_send.at[i],
            recv_sem=z_recv.at[slot],
            device_id=groups[2][i][2],
            device_id_type=MESH,
        )

    def z_start(to_elders):
        for i, (rank, own, _) in enumerate(groups[2]):

            @pl.when(rank < own if to_elders else rank > own)
            def _():
                z_copy(i).start()

    total = seq_sum()
    if n_dp == 16:
        xs[xi] = total
        await_younger(1)
        for i in range(3):
            x_copy(i).start()
    mix = lax.fori_loop(0, CHUNKS, fold, jnp.zeros((BLOCK, WIDE), f32))
    mean = jnp.broadcast_to(jnp.sum(mix, axis=1, keepdims=True) / D, (BLOCK, WIDE))

    if n_dp == 16:
        for i in range(3):
            x_arrival(i).wait_recv()
        zs[zi] = (xs[0] + xs[1]) + (xs[2] + xs[3])
        z_start(True)
    await_younger(3)
    lax.fori_loop(0, CHUNKS, finish, mean)
    lax.fori_loop(0, CHUNKS, forward_chunk, 0)
    if n_dp == 16:
        await_younger(2)
        z_start(False)
        for i in range(3):
            z_arrival(i).wait_recv()
        total = (zs[0] + zs[1]) + (zs[2] + zs[3])

    total = total * (1.0 / BATCH)
    gain, query_s, key_s, value_s = gains_of(me)
    for h in range(2):
        s = slice(h * HEAD_DIM, (h + 1) * HEAD_DIM)
        query_sum, key_sum, value_sum = (total[2 * i + h : 2 * i + h + 1, :] for i in range(3))
        sg_ref[0:1, s] = query_sum * query_s[:, s] + key_sum * key_s[:, s] + value_sum * value_s[:, s]
        sg_ref[1:2, s] = query_sum * gain[:, s]
        sg_ref[2:3, s] = key_sum * gain[:, s]
        sg_ref[3:4, s] = value_sum * gain[:, s]
        bg_ref[0:1, h : h + 1] = jnp.sum(total[6 + h : 7 + h, :], axis=1, keepdims=True)

    stat_copy.wait_send()
    if n_dp == 16:
        for i in range(3):
            x_copy(i).wait_send()
            z_copy(i).wait_send()
    for d in range(1, n_seq):
        peer = lax.rem(me + d, n_seq)
        part_copy(peer, peer, peer).wait_send()

    def drain(c, carry):
        saved_halo(c).wait_send()
        forward_halo(c).wait_send()
        fold_copy(c).wait_send()
        bwd_copy(c).wait()
        fwd_copy(c).wait()
        return carry

    lax.fori_loop(0, CHUNKS, drain, 0)


def hand_out(*refs):
    sources, targets, sems = refs[:4], refs[4:8], refs[8]
    copies = [pltpu.make_async_copy(sources[i], targets[i], sems.at[i]) for i in range(4)]
    for copy in copies:
        copy.start()
    for copy in copies:
        copy.wait()


def solution(mesh):
    sizes = tuple(mesh.shape[name] for name in ("dp", "pipe", "seq"))
    rows = (BLOCK, D)

    def on_device(fwd_input, saved_input, out_grad, fwd_sky, bwd_sky, norm_gain, query_scale, key_scale, value_scale, sky_bias):
        hbm = pl.BlockSpec(memory_space=pltpu.MemorySpace.HBM)
        vmem = pl.BlockSpec(memory_space=pltpu.MemorySpace.VMEM)
        smem = pl.BlockSpec(memory_space=pltpu.MemorySpace.SMEM)
        chunked = pltpu.VMEM((CHUNKS, BLOCK, WIDE), bf16)
        wide = pltpu.VMEM((BLOCK, WIDE), f32)
        window = pltpu.VMEM((2 * BLOCK, BLOCK), f32)
        tile = (8, 128)
        sem = pltpu.SemaphoreType.DMA
        results = ((rows, bf16), (rows, bf16), ((4, WIDE), f32), ((1, 2), f32))
        held = pl.pallas_call(
            functools.partial(kernel, sizes),
            out_shape=tuple(pltpu.VMEM(*result) for result in results),
            in_specs=[hbm] * 9 + [smem],
            out_specs=(vmem, vmem, vmem, vmem),
            scratch_shapes=[
                chunked, chunked, chunked,
                pltpu.VMEM((2 * CHUNKS, BLOCK, WIDE), bf16),
                chunked, chunked, chunked, chunked,
                pltpu.VMEM((CHUNKS, BLOCK, WIDE), f32),
                pltpu.VMEM((1, D), f32), pltpu.VMEM((1, D), f32), pltpu.VMEM((1, D), f32), pltpu.VMEM((1, D), f32),
                pltpu.VMEM((1, D // 2), jnp.int32), pltpu.VMEM((1, D // 2), jnp.int32),
                wide, wide, wide, wide, window, window, window,
                pltpu.VMEM(tile, f32), pltpu.VMEM(tile, f32),
                pltpu.VMEM((CHUNKS,) + tile, f32), pltpu.VMEM((CHUNKS,) + tile, f32),
                pltpu.VMEM((4,) + tile, f32), pltpu.VMEM((4,) + tile, f32),
                sem((3 * CHUNKS + 6,)), sem((2 * CHUNKS,)), sem((2 * CHUNKS,)), sem((CHUNKS,)), sem((CHUNKS,)),
                sem((2,)), sem((CHUNKS,)), sem((CHUNKS,)),
                sem((3,)), sem((4,)), sem((3,)), sem((4,)),
                sem((CHUNKS,)), sem((CHUNKS,)), sem((CHUNKS,)), sem((CHUNKS,)),
                pltpu.SemaphoreType.REGULAR((4,)),
            ],
            compiler_params=pltpu.CompilerParams(collective_id=0, has_side_effects=True),
            name="relay_tick",
        )(
            fwd_input.reshape(rows), saved_input.reshape(rows), out_grad.reshape(rows),
            fwd_sky.reshape(1, -1), bwd_sky.reshape(1, -1),
            norm_gain, query_scale, key_scale, value_scale, sky_bias,
        )
        fo, bo, sg, bg = pl.pallas_call(
            hand_out,
            out_shape=tuple(jax.ShapeDtypeStruct(*result) for result in results),
            in_specs=[pl.BlockSpec(memory_space=pl.ANY)] * 4,
            out_specs=(hbm,) * 4,
            scratch_shapes=[sem((4,))],
            name="hand_out",
        )(*(pltpu.with_memory_space_constraint(x, pltpu.MemorySpace.VMEM) for x in held))
        return fo[None, None], bo[None, None], sg[None], bg

    placed = (
        P("pipe", "dp", "seq", None),
        P("pipe", "dp", "seq", None),
        P("pipe", "dp", "seq", None),
        P("pipe", "dp", None),
        P("pipe", "dp", None),
        P("pipe", None),
        P("pipe", None),
        P("pipe", None),
        P("pipe", None),
        P("pipe", None),
    )
    return jax.shard_map(
        on_device,
        mesh=mesh,
        in_specs=placed,
        out_specs=(
            P("pipe", "dp", "seq", None),
            P("pipe", "dp", "seq", None),
            P("pipe", None, "seq"),
            P("pipe", "seq"),
        ),
        check_vma=False,
    )
```

```python
import functools
import math

import jax
import jax.numpy as jnp
from jax import lax
from jax.experimental import pallas as pl
from jax.experimental.pallas import tpu as pltpu
from jax.sharding import PartitionSpec as P

D = 2048
HEAD_DIM = 128
BATCH = 16
BLOCK = 128
WIDE = 256
CHUNKS = D // WIDE
AHEAD = 2

epsilon = 1e-05
factor = 1.0 / math.sqrt(HEAD_DIM)
f32 = jnp.float32
bf16 = jnp.bfloat16
MESH = pl.DeviceIdType.MESH


def dot(a, b, contract):
    return lax.dot_general(a, b, ((contract[:1], contract[1:]), ((), ())), preferred_element_type=f32)


def column_of(row):
    return jnp.transpose(jnp.broadcast_to(row, (BLOCK, BLOCK)))


def turn(i, at):
    if isinstance(i, int):
        return lax.rem(at + (2 * (i % 2) - 1) * ((CHUNKS - i) // 2) + CHUNKS, CHUNKS)
    return lax.rem(at + (2 * lax.rem(i, 2) - 1) * lax.div(CHUNKS - i, 2) + CHUNKS, CHUNKS)


def twice(square):
    return jnp.concatenate([square, square], axis=1)


def kernel(
    sizes,
    fx_ref, sx_ref, og_ref, fsky_ref, bsky_ref, ng_ref, qs_ref, ks_ref, vs_ref, bias_ref,
    fo_ref, bo_ref, sg_ref, bg_ref,
    sx, og, fx, halo, crecv, csend, bsend, fsend, grads,
    ng, qs, ks, vs, fsky, bsky,
    inv_s, inv_f, inv_sp, inv_fp, sky_s, sky_f, mask,
    stat_send, stat_recv, part_send, part_recv, xs, zs,
    load_sem, x_send, x_recv, c_send, c_recv, stat_sem, p_send, p_recv,
    xs_send, xs_recv, z_send, z_recv, fo_send, fo_recv, bo_send, bo_recv, hello,
):
    n_dp, n_pipe, n_seq = sizes
    me = lax.axis_index("seq")
    pipe = lax.axis_index("pipe")
    dp = lax.axis_index("dp")
    nxt, prv = lax.rem(me + 1, n_seq), lax.rem(me + n_seq - 1, n_seq)
    pnext, pprev = lax.rem(pipe + 1, n_pipe), lax.rem(pipe + n_pipe - 1, n_pipe)
    zi, xi = dp // 4, lax.rem(dp, 4)

    def ring_rank(i, n):
        return jnp.minimum(i, n - i) * n + i

    groups = [[], [], [], []]
    for d in range(2, n_seq - 1):
        peer = lax.rem(me + d, n_seq)
        groups[0].append((ring_rank(peer, n_seq), ring_rank(me, n_seq), {"seq": peer}))
    if n_dp == 16:
        for d in (1, 2, 3):
            peer = lax.rem(xi + d, 4)
            groups[1].append((ring_rank(peer, 4), ring_rank(xi, 4), {"dp": zi * 4 + peer}))
            peer = lax.rem(zi + d, 4)
            groups[2].append((peer, zi, {"dp": peer * 4 + xi}))
    for peer in (pnext, pprev):
        groups[3].append((peer, pipe, {"pipe": peer}))

    barrier = pltpu.get_barrier_semaphore()
    for peer in (nxt, prv):
        pl.semaphore_signal(barrier, inc=1, device_id={"seq": peer}, device_id_type=MESH)
    elders = 2
    for group in groups:
        for rank, own, peer in group:
            elders = elders + jnp.where(rank < own, 1, 0)

            @pl.when(rank > own)
            def _():
                pl.semaphore_signal(barrier, inc=1, device_id=peer, device_id_type=MESH)

    def await_younger(i):
        younger = sum(jnp.where(rank > own, 1, 0) for rank, own, _ in groups[i])

        @pl.when(younger > 0)
        def _():
            pl.semaphore_wait(hello.at[i], younger)

    def columns(c):
        return pl.ds(pl.multiple_of(c * WIDE, WIDE), WIDE)

    loads = []
    for source, target in ((sx_ref, sx), (fx_ref, fx), (og_ref, og)):
        for c in range(CHUNKS):
            loads.append((source.at[:, c * WIDE : (c + 1) * WIDE], target.at[c]))
    for source, target in (
        (ng_ref, ng), (qs_ref, qs), (ks_ref, ks), (vs_ref, vs), (fsky_ref, fsky), (bsky_ref, bsky),
    ):
        loads.append((source, target))
    copies = [pltpu.make_async_copy(a, b, load_sem.at[i]) for i, (a, b) in enumerate(loads)]
    for copy in copies:
        copy.start()

    def halo_copy(source, c, slot):
        return pltpu.make_async_remote_copy(
            src_ref=source.at[:, columns(c)],
            dst_ref=halo.at[slot],
            send_sem=x_send.at[slot],
            recv_sem=x_recv.at[slot],
            device_id={"seq": nxt},
            device_id_type=MESH,
        )

    def saved_halo(c):
        return halo_copy(sx_ref, c, c)

    def forward_halo(c):
        return halo_copy(fx_ref, c, c + CHUNKS)

    pl.semaphore_wait(barrier, elders)
    for i in range(AHEAD):
        saved_halo(turn(i, nxt)).start()
    for i, group in enumerate(groups):
        for rank, own, peer in group:

            @pl.when(rank < own)
            def _():
                pl.semaphore_signal(hello.at[i], inc=1, device_id=peer, device_id_type=MESH)

    def inverse_root(target):
        def add(c, total):
            rows = target[c].astype(f32)
            return total + rows * rows

        total = lax.fori_loop(0, CHUNKS, add, jnp.zeros((BLOCK, WIDE), f32))
        return lax.rsqrt(jnp.sum(total, axis=1, keepdims=True) / D + epsilon)

    for copy in copies[:CHUNKS]:
        copy.wait()
    inv = jnp.broadcast_to(inverse_root(sx), (BLOCK, BLOCK))
    inv_s[...] = twice(inv)
    stat_send[0:4, :] = jnp.transpose(inv)[0:4, :]
    for copy in copies[CHUNKS : 2 * CHUNKS]:
        copy.wait()
    inv = jnp.broadcast_to(inverse_root(fx), (BLOCK, BLOCK))
    inv_f[...] = twice(inv)
    stat_send[4:8, :] = jnp.transpose(inv)[0:4, :]
    stat_copy = pltpu.make_async_remote_copy(
        src_ref=stat_send,
        dst_ref=stat_recv,
        send_sem=stat_sem.at[0],
        recv_sem=stat_sem.at[1],
        device_id={"seq": nxt},
        device_id_type=MESH,
    )
    stat_copy.start()
    for i in range(AHEAD, CHUNKS):
        saved_halo(turn(i, nxt)).start()

    for copy in copies[2 * CHUNKS :]:
        copy.wait()

    for source, target in ((bsky, sky_s), (fsky, sky_f)):
        for half, block in ((0, prv), (1, me)):
            row = source[:, pl.ds(pl.multiple_of(block * BLOCK, BLOCK), BLOCK)].astype(f32)
            target[half * BLOCK : (half + 1) * BLOCK, :] = column_of(row)
    outer = lax.broadcasted_iota(jnp.int32, (2 * BLOCK, BLOCK), 0)
    inner = lax.broadcasted_iota(jnp.int32, (2 * BLOCK, BLOCK), 1)
    first_key = jnp.where(me > 0, 0, BLOCK)
    inside = (outer > inner) & (outer <= inner + BLOCK) & (outer >= first_key)
    mask[...] = jnp.where(inside, 0.0, -1e30).astype(f32)

    stat_copy.wait_recv()
    inv_sp[...] = twice(column_of(stat_recv[0:1, :]))
    inv_fp[...] = twice(column_of(stat_recv[4:5, :]))

    def gains_of(c):
        return tuple(r[:, columns(c)] for r in (ng, qs, ks, vs))

    def probabilities(key_window, query, head, sky):
        scores = dot(key_window, query, (1, 1)) * factor
        scores = scores + (bias_ref[0, head] * sky[...] + mask[...])
        top = jnp.max(scores, axis=0, keepdims=True)
        raised = jnp.exp(scores - top)
        return raised * (1.0 / jnp.sum(raised, axis=0, keepdims=True))

    def part_copy(c, slot, peer):
        return pltpu.make_async_remote_copy(
            src_ref=part_send.at[c],
            dst_ref=part_recv.at[slot],
            send_sem=p_send.at[c],
            recv_sem=p_recv.at[slot],
            device_id={"seq": peer},
            device_id_type=MESH,
        )

    def fold_copy(c):
        return pltpu.make_async_remote_copy(
            src_ref=csend.at[c],
            dst_ref=crecv.at[c],
            send_sem=c_send.at[c],
            recv_sem=c_recv.at[c],
            device_id={"seq": prv},
            device_id_type=MESH,
        )

    def backward_chunk(i, carry):
        c = turn(i, me)
        saved_halo(c).wait_recv()
        gain, query_s, key_s, value_s = gains_of(c)
        scaled = sx[c].astype(f32) * inv_s[...]
        normed = scaled * gain
        query = (normed * query_s).astype(bf16)
        key = (normed * key_s).astype(bf16)
        value = (normed * value_s).astype(bf16)
        scaled_p = halo[c].astype(f32) * inv_sp[...]
        normed_p = scaled_p * gain
        key_p = (normed_p * key_s).astype(bf16)
        value_p = (normed_p * value_s).astype(bf16)
        upstream = og[c]
        query_grads, key_grads, value_grads, biases = [], [], [], []
        for h in range(2):
            s = slice(h * HEAD_DIM, (h + 1) * HEAD_DIM)
            query_h, upstream_h = query[:, s], upstream[:, s]
            key_window = jnp.concatenate([key_p[:, s], key[:, s]], axis=0)
            value_window = jnp.concatenate([value_p[:, s], value[:, s]], axis=0)
            probs = probabilities(key_window, query_h, 2 * c + h, sky_s)
            value_grads.append(dot(probs.astype(bf16), upstream_h, (1, 0)))
            prob_grad = dot(value_window, upstream_h, (1, 1))
            score_grad = probs * (prob_grad - jnp.sum(probs * prob_grad, axis=0, keepdims=True))
            biases.append(jnp.sum(score_grad * sky_s[...], axis=0, keepdims=True))
            score_low = score_grad.astype(bf16)
            key_grads.append(dot(score_low, query_h, (1, 0)) * factor)
            query_grads.append(dot(score_low, key_window, (0, 0)) * factor)
        query_grad = jnp.concatenate(query_grads, axis=1).astype(bf16).astype(f32)
        key_grad = jnp.concatenate(key_grads, axis=1)
        value_grad = jnp.concatenate(value_grads, axis=1)
        key_b, key_a = key_grad[:BLOCK], key_grad[BLOCK:]
        value_b, value_a = value_grad[:BLOCK], value_grad[BLOCK:]
        csend[c] = (key_b * key_s + value_b * value_s).astype(bf16)
        fold_copy(c).start()
        grads[c] = query_grad * query_s + key_a * key_s + value_a * value_s
        sums = (
            jnp.sum(query_grad * scaled, axis=0, keepdims=True),
            jnp.sum(key_a * scaled + key_b * scaled_p, axis=0, keepdims=True),
            jnp.sum(value_a * scaled + value_b * scaled_p, axis=0, keepdims=True),
        )
        for j, row in enumerate(sums):
            part_send[c, 2 * j : 2 * j + 1, :] = row[:, :HEAD_DIM]
            part_send[c, 2 * j + 1 : 2 * j + 2, :] = row[:, HEAD_DIM:]
        part_send[c, 6:7, :] = biases[0]
        part_send[c, 7:8, :] = biases[1]

        @pl.when(i == 1)
        def _():
            await_younger(0)
            first = turn(0, me)
            part_copy(first, me, first).start()

        @pl.when((i >= 1) & (i < CHUNKS - 1))
        def _():
            part_copy(c, me, c).start()

        @pl.when(i == CHUNKS - 2)
        def _():
            for later in range(CHUNKS):
                forward_halo(later).start()

        return carry

    lax.fori_loop(0, CHUNKS, backward_chunk, 0)

    def fold(c, total):
        fold_copy(c).wait_recv()
        scaled_grad = (grads[c] + crecv[c].astype(f32)) * ng[:, columns(c)]
        grads[c] = scaled_grad
        return total + scaled_grad * (sx[c].astype(f32) * inv_s[...])

    def bwd_copy(c):
        return pltpu.make_async_remote_copy(
            src_ref=bsend.at[c],
            dst_ref=bo_ref.at[:, columns(c)],
            send_sem=bo_send.at[c],
            recv_sem=bo_recv.at[c],
            device_id={"pipe": pprev},
            device_id_type=MESH,
        )

    def finish(c, carry):
        root = inv_s[...]
        scaled = sx[c].astype(f32) * root
        bsend[c] = (og[c].astype(f32) + root * (grads[c] - scaled * carry)).astype(bf16)
        bwd_copy(c).start()
        return carry

    def fwd_copy(c):
        return pltpu.make_async_remote_copy(
            src_ref=fsend.at[c],
            dst_ref=fo_ref.at[:, columns(c)],
            send_sem=fo_send.at[c],
            recv_sem=fo_recv.at[c],
            device_id={"pipe": pnext},
            device_id_type=MESH,
        )

    def forward_chunk(c, carry):
        forward_halo(c).wait_recv()
        gain, query_s, key_s, value_s = gains_of(c)
        rows = fx[c].astype(f32)
        normed = rows * inv_f[...] * gain
        query = (normed * query_s).astype(bf16)
        key = (normed * key_s).astype(bf16)
        value = (normed * value_s).astype(bf16)
        normed_p = halo[c + CHUNKS].astype(f32) * inv_fp[...] * gain
        key_p = (normed_p * key_s).astype(bf16)
        value_p = (normed_p * value_s).astype(bf16)
        attended = []
        for h in range(2):
            s = slice(h * HEAD_DIM, (h + 1) * HEAD_DIM)
            key_window = jnp.concatenate([key_p[:, s], key[:, s]], axis=0)
            value_window = jnp.concatenate([value_p[:, s], value[:, s]], axis=0)
            probs = probabilities(key_window, query[:, s], 2 * c + h, sky_f).astype(bf16)
            attended.append(dot(probs, value_window, (0, 0)))
        attended = jnp.concatenate(attended, axis=1).astype(bf16).astype(f32)
        fsend[c] = (rows + attended).astype(bf16)
        fwd_copy(c).start()
        return carry

    def seq_sum():
        total = part_send[me]
        for d in range(1, n_seq):
            peer = lax.rem(me + d, n_seq)
            part_copy(peer, peer, peer).wait_recv()
            total = total + part_recv[peer]
        return total

    def x_copy(i):
        return pltpu.make_async_remote_copy(
            src_ref=xs.at[xi],
            dst_ref=xs.at[xi],
            send_sem=xs_send.at[i],
            recv_sem=xs_recv.at[xi],
            device_id=groups[1][i][2],
            device_id_type=MESH,
        )

    def x_arrival(i):
        slot = lax.rem(xi + i + 1, 4)
        return pltpu.make_async_remote_copy(
            src_ref=xs.at[slot],
            dst_ref=xs.at[slot],
            send_sem=xs_send.at[i],
            recv_sem=xs_recv.at[slot],
            device_id=groups[1][i][2],
            device_id_type=MESH,
        )

    def z_copy(i):
        return pltpu.make_async_remote_copy(
            src_ref=zs.at[zi],
            dst_ref=zs.at[zi],
            send_sem=z_send.at[i],
            recv_sem=z_recv.at[zi],
            device_id=groups[2][i][2],
            device_id_type=MESH,
        )

    def z_arrival(i):
        slot = lax.rem(zi + i + 1, 4)
        return pltpu.make_async_remote_copy(
            src_ref=zs.at[slot],
            dst_ref=zs.at[slot],
            send_sem=z_send.at[i],
            recv_sem=z_recv.at[slot],
            device_id=groups[2][i][2],
            device_id_type=MESH,
        )

    def z_start(to_elders):
        for i, (rank, own, _) in enumerate(groups[2]):

            @pl.when(rank < own if to_elders else rank > own)
            def _():
                z_copy(i).start()

    total = seq_sum()
    if n_dp == 16:
        xs[xi] = total
        await_younger(1)
        for i in range(3):
            x_copy(i).start()
    mix = lax.fori_loop(0, CHUNKS, fold, jnp.zeros((BLOCK, WIDE), f32))
    mean = jnp.broadcast_to(jnp.sum(mix, axis=1, keepdims=True) / D, (BLOCK, WIDE))

    if n_dp == 16:
        for i in range(3):
            x_arrival(i).wait_recv()
        zs[zi] = (xs[0] + xs[1]) + (xs[2] + xs[3])
        z_start(True)
    await_younger(3)
    lax.fori_loop(0, CHUNKS, finish, mean)
    lax.fori_loop(0, CHUNKS, forward_chunk, 0)
    if n_dp == 16:
        await_younger(2)
        z_start(False)
        for i in range(3):
            z_arrival(i).wait_recv()
        total = (zs[0] + zs[1]) + (zs[2] + zs[3])

    total = total * (1.0 / BATCH)
    gain, query_s, key_s, value_s = gains_of(me)
    for h in range(2):
        s = slice(h * HEAD_DIM, (h + 1) * HEAD_DIM)
        query_sum, key_sum, value_sum = (total[2 * i + h : 2 * i + h + 1, :] for i in range(3))
        sg_ref[0:1, s] = query_sum * query_s[:, s] + key_sum * key_s[:, s] + value_sum * value_s[:, s]
        sg_ref[1:2, s] = query_sum * gain[:, s]
        sg_ref[2:3, s] = key_sum * gain[:, s]
        sg_ref[3:4, s] = value_sum * gain[:, s]
        bg_ref[0:1, h : h + 1] = jnp.sum(total[6 + h : 7 + h, :], axis=1, keepdims=True)

    stat_copy.wait_send()
    if n_dp == 16:
        for i in range(3):
            x_copy(i).wait_send()
            z_copy(i).wait_send()
    for d in range(1, n_seq):
        peer = lax.rem(me + d, n_seq)
        part_copy(peer, peer, peer).wait_send()

    def drain(c, carry):
        saved_halo(c).wait_send()
        forward_halo(c).wait_send()
        fold_copy(c).wait_send()
        bwd_copy(c).wait()
        fwd_copy(c).wait()
        return carry

    lax.fori_loop(0, CHUNKS, drain, 0)


def hand_out(*refs):
    sources, targets, sems = refs[:4], refs[4:8], refs[8]
    copies = [pltpu.make_async_copy(sources[i], targets[i], sems.at[i]) for i in range(4)]
    for copy in copies:
        copy.start()
    for copy in copies:
        copy.wait()


def solution(mesh):
    sizes = tuple(mesh.shape[name] for name in ("dp", "pipe", "seq"))
    rows = (BLOCK, D)

    def on_device(fwd_input, saved_input, out_grad, fwd_sky, bwd_sky, norm_gain, query_scale, key_scale, value_scale, sky_bias):
        hbm = pl.BlockSpec(memory_space=pltpu.MemorySpace.HBM)
        vmem = pl.BlockSpec(memory_space=pltpu.MemorySpace.VMEM)
        smem = pl.BlockSpec(memory_space=pltpu.MemorySpace.SMEM)
        chunked = pltpu.VMEM((CHUNKS, BLOCK, WIDE), bf16)
        wide = pltpu.VMEM((BLOCK, WIDE), f32)
        window = pltpu.VMEM((2 * BLOCK, BLOCK), f32)
        tile = (8, 128)
        sem = pltpu.SemaphoreType.DMA
        results = ((rows, bf16), (rows, bf16), ((4, WIDE), f32), ((1, 2), f32))
        held = pl.pallas_call(
            functools.partial(kernel, sizes),
            out_shape=tuple(pltpu.VMEM(*result) for result in results),
            in_specs=[hbm] * 9 + [smem],
            out_specs=(vmem, vmem, vmem, vmem),
            scratch_shapes=[
                chunked, chunked, chunked,
                pltpu.VMEM((2 * CHUNKS, BLOCK, WIDE), bf16),
                chunked, chunked, chunked, chunked,
                pltpu.VMEM((CHUNKS, BLOCK, WIDE), f32),
                pltpu.VMEM((1, D), f32), pltpu.VMEM((1, D), f32), pltpu.VMEM((1, D), f32), pltpu.VMEM((1, D), f32),
                pltpu.VMEM((1, D // 2), jnp.int32), pltpu.VMEM((1, D // 2), jnp.int32),
                wide, wide, wide, wide, window, window, window,
                pltpu.VMEM(tile, f32), pltpu.VMEM(tile, f32),
                pltpu.VMEM((CHUNKS,) + tile, f32), pltpu.VMEM((CHUNKS,) + tile, f32),
                pltpu.VMEM((4,) + tile, f32), pltpu.VMEM((4,) + tile, f32),
                sem((3 * CHUNKS + 6,)), sem((2 * CHUNKS,)), sem((2 * CHUNKS,)), sem((CHUNKS,)), sem((CHUNKS,)),
                sem((2,)), sem((CHUNKS,)), sem((CHUNKS,)),
                sem((3,)), sem((4,)), sem((3,)), sem((4,)),
                sem((CHUNKS,)), sem((CHUNKS,)), sem((CHUNKS,)), sem((CHUNKS,)),
                pltpu.SemaphoreType.REGULAR((4,)),
            ],
            compiler_params=pltpu.CompilerParams(collective_id=0, has_side_effects=True),
            name="relay_tick",
        )(
            fwd_input.reshape(rows), saved_input.reshape(rows), out_grad.reshape(rows),
            fwd_sky.reshape(1, -1), bwd_sky.reshape(1, -1),
            norm_gain, query_scale, key_scale, value_scale, sky_bias,
        )
        fo, bo, sg, bg = pl.pallas_call(
            hand_out,
            out_shape=tuple(jax.ShapeDtypeStruct(*result) for result in results),
            in_specs=[pl.BlockSpec(memory_space=pl.ANY)] * 4,
            out_specs=(hbm,) * 4,
            scratch_shapes=[sem((4,))],
            name="hand_out",
        )(*(pltpu.with_memory_space_constraint(x, pltpu.MemorySpace.VMEM) for x in held))
        return fo[None, None], bo[None, None], sg[None], bg

    placed = (
        P("pipe", "dp", "seq", None),
        P("pipe", "dp", "seq", None),
        P("pipe", "dp", "seq", None),
        P("pipe", "dp", None),
        P("pipe", "dp", None),
        P("pipe", None),
        P("pipe", None),
        P("pipe", None),
        P("pipe", None),
        P("pipe", None),
    )
    return jax.shard_map(
        on_device,
        mesh=mesh,
        in_specs=placed,
        out_specs=(
            P("pipe", "dp", "seq", None),
            P("pipe", "dp", "seq", None),
            P("pipe", None, "seq"),
            P("pipe", "seq"),
        ),
        check_vma=False,
    )
```
